256 devices in a mesh: rows: 32 (over y, z), cols: 8 (over x, core).
Axes of the slice: x: 4, y: 4, z: 8, core: 2. Of those that a mesh axis runs over, the one named last changes fastest.
Arguments:
- snapshots: bfloat16 [524288, 2048], P(('rows', 'cols')), may hold values from -24 to 24
- test_matrix: bfloat16 [2048, 256], replicated, may hold values from -0.125 to 0.125
Outputs:
- basis: float32 [524288, 256], P(('rows', 'cols'))
- coeffs: float32 [256, 2048], P('rows', 'cols')
The draws below stay inside these ranges and needn't reach their ends.
All inputs are finite; a program needn't handle non-finite values.
Results may differ from the reference program's by a relative error of at most 0.0005.
Values sent between devices are 32-bit elements; how exact they have to be, the bound alone decides.
A program may use at most 64 MiB of HBM per device.

```python
import math
import jax
import jax.numpy as jnp
from jax import lax

NCOL = 2048
RANK = 256
NROWS = 524288


def draw_snapshots(key, part):
    key_base, key_rough = jax.random.split(jax.random.fold_in(key, 11), 2)
    position = jnp.arange(NROWS, dtype=jnp.float32) / NROWS
    rough = jnp.exp(jax.random.uniform(key_rough, (NROWS, 1), jnp.float32, 0.0, math.log(2.0)))
    row_scale = jnp.exp(position[:, None] * math.log(3.0)) * rough
    base = jnp.clip(jax.random.normal(key_base, (NROWS, NCOL), jnp.float32), -4.0, 4.0)
    return (base * row_scale).astype(jnp.bfloat16)


def bell_draw(stream_key, extent, scale, limit, kind=jnp.bfloat16):
    array = scale * jax.random.normal(stream_key, extent, jnp.float32)
    return jnp.clip(array, min=-limit, max=limit).astype(kind)


def setup_inputs(seed: int = 0) -> dict:
    keys = jax.random.split(jax.random.key(seed), 3)
    return {
        "snapshots": draw_snapshots(jax.random.fold_in(keys[2], 71), 0),
        "test_matrix": bell_draw(keys[1], (NCOL, RANK), NCOL ** -0.5, 0.125),
    }


def reference(snapshots, test_matrix):
    sketch = jnp.dot(snapshots.astype(jnp.float32), test_matrix.astype(jnp.float32), preferred_element_type=jnp.float32)
    q_factor, r_factor = jnp.linalg.qr(sketch)
    diag_values = jnp.diagonal(r_factor)
    signs = jnp.where(diag_values < 0, -1.0, 1.0).astype(q_factor.dtype)
    basis = q_factor * signs[None, :] * math.sqrt(NROWS)
    basis_half = basis.astype(jnp.bfloat16)
    projected = lax.dot_general(basis_half.astype(jnp.float32), snapshots.astype(jnp.float32), (((0,), (0,)), ((), ())), preferred_element_type=jnp.float32)
    coeffs = projected * (1.0 / math.sqrt(NROWS))
    return (basis, coeffs)
```

```python
import math

import jax
import jax.numpy as jnp
from jax import lax
from jax.sharding import PartitionSpec as P


def cross_product(left, right):
    return lax.dot_general(
        left,
        right,
        (((0,), (0,)), ((), ())),
        precision=lax.Precision.HIGHEST,
        preferred_element_type=jnp.float32,
    )


def lower_inverse(gram):
    lower = jnp.linalg.cholesky(gram)
    identity = jnp.eye(gram.shape[0], dtype=gram.dtype)
    return jax.scipy.linalg.solve_triangular(lower, identity, lower=True)


def reduce_scatter(x, axis, n):
    chunks = x.reshape(n, x.shape[0] // n, *x.shape[1:])
    return lax.all_to_all(chunks, axis, 0, 0, tiled=True).sum(0)


def all_reduce(x):
    axes = ("rows", "cols")
    n = lax.axis_size(axes)
    mine = reduce_scatter(x, axes, n)
    spread = jnp.broadcast_to(mine[None], (n, *mine.shape))
    return lax.all_to_all(spread, axes, 0, 0, tiled=True).reshape(x.shape)


def body(snapshots, test_matrix):
    n_rows = lax.axis_size("rows")
    n_cols = lax.axis_size("cols")
    rows_here = snapshots.shape[0]
    total_rows = rows_here * n_rows * n_cols
    sketch = jnp.dot(snapshots, test_matrix, preferred_element_type=jnp.float32)
    gram_local = cross_product(sketch, sketch)
    summed = all_reduce(gram_local)
    inverse_low = lower_inverse(summed)
    basis_full = lax.dot_general(
        sketch,
        inverse_low,
        (((1,), (1,)), ((), ())),
        precision=lax.Precision.HIGHEST,
        preferred_element_type=jnp.float32,
    ) * math.sqrt(total_rows)
    basis_half = basis_full.astype(jnp.bfloat16)
    partial = lax.dot_general(
        snapshots, basis_half, (((0,), (0,)), ((), ())), preferred_element_type=jnp.float32
    )
    grid_part = reduce_scatter(partial, "cols", n_cols)
    projected = reduce_scatter(grid_part.T, "rows", n_rows)
    coeffs = projected * (1.0 / math.sqrt(total_rows))
    return (basis_full, coeffs)


def solution(mesh):
    placed = (P(("rows", "cols"), None), P())
    return jax.shard_map(
        body,
        mesh=mesh,
        in_specs=placed,
        out_specs=(P(("rows", "cols"), None), P("rows", "cols")),
        check_vma=False,
    )
```

```python
import math

import jax
import jax.numpy as jnp
from jax import lax
from jax.sharding import PartitionSpec as P


def cross_product(left, right):
    return lax.dot_general(
        left,
        right,
        (((0,), (0,)), ((), ())),
        precision=lax.Precision.HIGHEST,
        preferred_element_type=jnp.float32,
    )


def matmul(left, right):
    return jnp.dot(left, right, precision=lax.Precision.HIGHEST, preferred_element_type=jnp.float32)


def lower_inverse(gram):
    half = gram.shape[0] // 2
    identity = jnp.eye(half, dtype=gram.dtype)
    low11 = jnp.linalg.cholesky(gram[:half, :half])
    inv11 = lax.linalg.triangular_solve(low11, identity, left_side=True, lower=True)
    low21 = matmul(gram[half:, :half], inv11.T)
    low22 = jnp.linalg.cholesky(gram[half:, half:] - matmul(low21, low21.T))
    inv22 = lax.linalg.triangular_solve(low22, identity, left_side=True, lower=True)
    inv21 = -matmul(inv22, matmul(low21, inv11))
    top = jnp.concatenate([inv11, jnp.zeros_like(inv11)], axis=1)
    return jnp.concatenate([top, jnp.concatenate([inv21, inv22], axis=1)], axis=0)


def reduce_scatter(x, axis, n):
    chunks = x.reshape(n, x.shape[0] // n, *x.shape[1:])
    return lax.all_to_all(chunks, axis, 0, 0, tiled=True).sum(0)


def all_reduce(x):
    axes = ("rows", "cols")
    n = lax.axis_size(axes)
    mine = reduce_scatter(x, axes, n)
    spread = jnp.broadcast_to(mine[None], (n, *mine.shape))
    return lax.all_to_all(spread, axes, 0, 0, tiled=True).reshape(x.shape)


def body(snapshots, test_matrix):
    n_rows = lax.axis_size("rows")
    n_cols = lax.axis_size("cols")
    rows_here = snapshots.shape[0]
    total_rows = rows_here * n_rows * n_cols
    sketch = jnp.dot(snapshots, test_matrix, preferred_element_type=jnp.float32)
    gram_local = cross_product(sketch, sketch)
    summed = all_reduce(gram_local)
    inverse_low = lower_inverse(summed)
    basis_full = lax.dot_general(
        sketch,
        inverse_low,
        (((1,), (1,)), ((), ())),
        precision=lax.Precision.HIGHEST,
        preferred_element_type=jnp.float32,
    ) * math.sqrt(total_rows)
    basis_half = basis_full.astype(jnp.bfloat16)
    partial = lax.dot_general(
        snapshots, basis_half, (((0,), (0,)), ((), ())), preferred_element_type=jnp.float32
    )
    grid_part = reduce_scatter(partial, "cols", n_cols)
    projected = reduce_scatter(grid_part.T, "rows", n_rows)
    coeffs = projected * (1.0 / math.sqrt(total_rows))
    return (basis_full, coeffs)


def solution(mesh):
    placed = (P(("rows", "cols"), None), P())
    return jax.shard_map(
        body,
        mesh=mesh,
        in_specs=placed,
        out_specs=(P(("rows", "cols"), None), P("rows", "cols")),
        check_vma=False,
    )
```

```python
import functools
import math

import jax
import jax.numpy as jnp
from jax import lax
from jax.experimental import pallas as pl
from jax.experimental.pallas import tpu as pltpu
from jax.sharding import PartitionSpec as P


def cross_product(left, right):
    return lax.dot_general(
        left,
        right,
        (((0,), (0,)), ((), ())),
        precision=lax.Precision.HIGHEST,
        preferred_element_type=jnp.float32,
    )


def matmul(left, right):
    return jnp.dot(left, right, precision=lax.Precision.HIGHEST, preferred_element_type=jnp.float32)


def lower_inverse(gram):
    half = gram.shape[0] // 2
    identity = jnp.eye(half, dtype=gram.dtype)
    low11 = jnp.linalg.cholesky(gram[:half, :half])
    inv11 = lax.linalg.triangular_solve(low11, identity, left_side=True, lower=True)
    low21 = matmul(gram[half:, :half], inv11.T)
    low22 = jnp.linalg.cholesky(gram[half:, half:] - matmul(low21, low21.T))
    inv22 = lax.linalg.triangular_solve(low22, identity, left_side=True, lower=True)
    inv21 = -matmul(inv22, matmul(low21, inv11))
    top = jnp.concatenate([inv11, jnp.zeros_like(inv11)], axis=1)
    return jnp.concatenate([top, jnp.concatenate([inv21, inv22], axis=1)], axis=0)


def reduce_scatter(x, axis, n):
    chunks = x.reshape(n, x.shape[0] // n, *x.shape[1:])
    return lax.all_to_all(chunks, axis, 0, 0, tiled=True).sum(0)


def all_reduce_kernel(n_cols, n, local_ref, out_ref, recv, mine, send1, recv1, send2, recv2):
    me = lax.axis_index("rows") * n_cols + lax.axis_index("cols")

    def device(p):
        return (p // n_cols, p % n_cols)

    def peers(step):
        def visit(i, carry):
            p = lax.rem(me + 1 + i, n)
            step(p)
            return carry

        lax.fori_loop(0, n - 1, visit, 0)

    barrier = pltpu.get_barrier_semaphore()

    def greet(p):
        pl.semaphore_signal(barrier, inc=1, device_id=device(p), device_id_type=pl.DeviceIdType.MESH)

    peers(greet)
    pl.semaphore_wait(barrier, n - 1)

    def scatter_copy(p):
        return pltpu.make_async_remote_copy(
            src_ref=local_ref.at[p],
            dst_ref=recv.at[me],
            send_sem=send1.at[p],
            recv_sem=recv1.at[me],
            device_id=device(p),
            device_id_type=pl.DeviceIdType.MESH,
        )

    def arrived(sem, buffer, p):
        return pltpu.make_async_remote_copy(
            src_ref=buffer.at[p],
            dst_ref=buffer.at[p],
            send_sem=sem.at[p],
            recv_sem=sem.at[p],
            device_id=device(p),
            device_id_type=pl.DeviceIdType.MESH,
        )

    peers(lambda p: scatter_copy(p).start())
    recv[me] = local_ref[me]
    peers(lambda p: arrived(recv1, recv, p).wait_recv())
    peers(lambda p: scatter_copy(p).wait_send())
    mine[...] = jnp.sum(recv[...], axis=0)

    def gather_copy(p):
        return pltpu.make_async_remote_copy(
            src_ref=mine,
            dst_ref=out_ref.at[me],
            send_sem=send2.at[p],
            recv_sem=recv2.at[me],
            device_id=device(p),
            device_id_type=pl.DeviceIdType.MESH,
        )

    peers(lambda p: gather_copy(p).start())
    out_ref[me] = mine[...]
    peers(lambda p: arrived(recv2, out_ref, p).wait_recv())
    peers(lambda p: gather_copy(p).wait_send())


def all_reduce(x):
    n_cols = lax.axis_size("cols")
    n = lax.axis_size("rows") * n_cols
    rows, width = x.shape
    block = (n, rows // n, width)
    out = pl.pallas_call(
        functools.partial(all_reduce_kernel, n_cols, n),
        out_shape=jax.ShapeDtypeStruct(block, x.dtype),
        in_specs=[pl.BlockSpec(memory_space=pltpu.VMEM)],
        out_specs=pl.BlockSpec(memory_space=pltpu.VMEM),
        scratch_shapes=[
            pltpu.VMEM(block, x.dtype),
            pltpu.VMEM(block[1:], x.dtype),
            pltpu.SemaphoreType.DMA((n,)),
            pltpu.SemaphoreType.DMA((n,)),
            pltpu.SemaphoreType.DMA((n,)),
            pltpu.SemaphoreType.DMA((n,)),
        ],
        compiler_params=pltpu.CompilerParams(collective_id=0, has_side_effects=True),
    )(x.reshape(block))
    return out.reshape(rows, width)


def body(snapshots, test_matrix):
    n_rows = lax.axis_size("rows")
    n_cols = lax.axis_size("cols")
    rows_here = snapshots.shape[0]
    total_rows = rows_here * n_rows * n_cols
    sketch = jnp.dot(snapshots, test_matrix, preferred_element_type=jnp.float32)
    gram_local = cross_product(sketch, sketch)
    summed = all_reduce(gram_local)
    inverse_low = lower_inverse(summed)
    basis_full = lax.dot_general(
        sketch,
        inverse_low,
        (((1,), (1,)), ((), ())),
        precision=lax.Precision.HIGHEST,
        preferred_element_type=jnp.float32,
    ) * math.sqrt(total_rows)
    basis_half = basis_full.astype(jnp.bfloat16)
    partial = lax.dot_general(
        snapshots, basis_half, (((0,), (0,)), ((), ())), preferred_element_type=jnp.float32
    )
    grid_part = reduce_scatter(partial, "cols", n_cols)
    projected = reduce_scatter(grid_part.T, "rows", n_rows)
    coeffs = projected * (1.0 / math.sqrt(total_rows))
    return (basis_full, coeffs)


def solution(mesh):
    placed = (P(("rows", "cols"), None), P())
    return jax.shard_map(
        body,
        mesh=mesh,
        in_specs=placed,
        out_specs=(P(("rows", "cols"), None), P("rows", "cols")),
        check_vma=False,
    )
```

```python
import functools
import math

import jax
import jax.numpy as jnp
from jax import lax
from jax.experimental import pallas as pl
from jax.experimental.pallas import tpu as pltpu
from jax.sharding import PartitionSpec as P


def cross_product(left, right):
    return lax.dot_general(
        left,
        right,
        (((0,), (0,)), ((), ())),
        precision=lax.Precision.HIGHEST,
        preferred_element_type=jnp.float32,
    )


def matmul(left, right):
    return jnp.dot(left, right, precision=lax.Precision.HIGHEST, preferred_element_type=jnp.float32)


def lower_inverse(gram):
    half = gram.shape[0] // 2
    identity = jnp.eye(half, dtype=gram.dtype)
    low11 = jnp.linalg.cholesky(gram[:half, :half])
    inv11 = lax.linalg.triangular_solve(low11, identity, left_side=True, lower=True)
    low21 = matmul(gram[half:, :half], inv11.T)
    low22 = jnp.linalg.cholesky(gram[half:, half:] - matmul(low21, low21.T))
    inv22 = lax.linalg.triangular_solve(low22, identity, left_side=True, lower=True)
    inv21 = -matmul(inv22, matmul(low21, inv11))
    top = jnp.concatenate([inv11, jnp.zeros_like(inv11)], axis=1)
    return jnp.concatenate([top, jnp.concatenate([inv21, inv22], axis=1)], axis=0)


def reduce_scatter(x, axis, n):
    chunks = x.reshape(n, x.shape[0] // n, *x.shape[1:])
    return lax.all_to_all(chunks, axis, 0, 0, tiled=True).sum(0)


def all_reduce_kernel(n_rows, n_cols, local_ref, out_ref, recv1, part, recv2, total,
                      send1, arrive1, send2, arrive2, send3, arrive3, send4, arrive4):
    me_r = lax.axis_index("rows")
    me_c = lax.axis_index("cols")

    def along(n, mine, step):
        def visit(i, carry):
            step(lax.rem(mine + 1 + i, n))
            return carry

        lax.fori_loop(0, n - 1, visit, 0)

    def copy(src, dst, send, arrive, device):
        return pltpu.make_async_remote_copy(
            src_ref=src, dst_ref=dst, send_sem=send, recv_sem=arrive,
            device_id=device, device_id_type=pl.DeviceIdType.MESH,
        )

    barrier = pltpu.get_barrier_semaphore()
    along(n_cols, me_c, lambda c: pl.semaphore_signal(
        barrier, inc=1, device_id=(me_r, c), device_id_type=pl.DeviceIdType.MESH))
    along(n_rows, me_r, lambda r: pl.semaphore_signal(
        barrier, inc=1, device_id=(r, me_c), device_id_type=pl.DeviceIdType.MESH))
    pl.semaphore_wait(barrier, n_cols + n_rows - 2)

    def scatter1(c):
        return copy(local_ref.at[c], recv1.at[me_c], send1.at[c], arrive1.at[me_c], (me_r, c))

    along(n_cols, me_c, lambda c: scatter1(c).start())
    recv1[me_c] = local_ref[me_c]
    along(n_cols, me_c, lambda c: copy(recv1.at[c], recv1.at[c], send1.at[c], arrive1.at[c], (me_r, c)).wait_recv())
    along(n_cols, me_c, lambda c: scatter1(c).wait_send())
    summed = jnp.sum(recv1[...], axis=0)
    share = part.shape[1]
    for r in range(n_rows):
        part[r] = summed[r * share:(r + 1) * share]

    def scatter2(r):
        return copy(part.at[r], recv2.at[me_r], send2.at[r], arrive2.at[me_r], (r, me_c))

    along(n_rows, me_r, lambda r: scatter2(r).start())
    recv2[me_r] = part[me_r]
    along(n_rows, me_r, lambda r: copy(recv2.at[r], recv2.at[r], send2.at[r], arrive2.at[r], (r, me_c)).wait_recv())
    along(n_rows, me_r, lambda r: scatter2(r).wait_send())
    total[...] = jnp.sum(recv2[...], axis=0)

    def gather3(r):
        return copy(total, out_ref.at[me_c, me_r], send3.at[r], arrive3.at[me_r], (r, me_c))

    along(n_rows, me_r, lambda r: gather3(r).start())
    out_ref[me_c, me_r] = total[...]
    along(n_rows, me_r, lambda r: copy(out_ref.at[me_c, r], out_ref.at[me_c, r], send3.at[r], arrive3.at[r], (r, me_c)).wait_recv())
    along(n_rows, me_r, lambda r: gather3(r).wait_send())

    def gather4(c):
        return copy(out_ref.at[me_c], out_ref.at[me_c], send4.at[c], arrive4.at[me_c], (me_r, c))

    along(n_cols, me_c, lambda c: gather4(c).start())
    along(n_cols, me_c, lambda c: copy(out_ref.at[c], out_ref.at[c], send4.at[c], arrive4.at[c], (me_r, c)).wait_recv())
    along(n_cols, me_c, lambda c: gather4(c).wait_send())


def all_reduce(x):
    n_rows = lax.axis_size("rows")
    n_cols = lax.axis_size("cols")
    rows, width = x.shape
    block = rows // n_cols
    out = pl.pallas_call(
        functools.partial(all_reduce_kernel, n_rows, n_cols),
        out_shape=jax.ShapeDtypeStruct((n_cols, n_rows, block // n_rows, width), x.dtype),
        in_specs=[pl.BlockSpec(memory_space=pltpu.VMEM)],
        out_specs=pl.BlockSpec(memory_space=pltpu.VMEM),
        scratch_shapes=[
            pltpu.VMEM((n_cols, block, width), x.dtype),
            pltpu.VMEM((n_rows, block // n_rows, width), x.dtype),
            pltpu.VMEM((n_rows, block // n_rows, width), x.dtype),
            pltpu.VMEM((block // n_rows, width), x.dtype),
            pltpu.SemaphoreType.DMA((n_cols,)),
            pltpu.SemaphoreType.DMA((n_cols,)),
            pltpu.SemaphoreType.DMA((n_rows,)),
            pltpu.SemaphoreType.DMA((n_rows,)),
            pltpu.SemaphoreType.DMA((n_rows,)),
            pltpu.SemaphoreType.DMA((n_rows,)),
            pltpu.SemaphoreType.DMA((n_cols,)),
            pltpu.SemaphoreType.DMA((n_cols,)),
        ],
        compiler_params=pltpu.CompilerParams(collective_id=0, has_side_effects=True),
    )(x.reshape(n_cols, block, width))
    return out.reshape(rows, width)


def body(snapshots, test_matrix):
    n_rows = lax.axis_size("rows")
    n_cols = lax.axis_size("cols")
    rows_here = snapshots.shape[0]
    total_rows = rows_here * n_rows * n_cols
    sketch = jnp.dot(snapshots, test_matrix, preferred_element_type=jnp.float32)
    gram_local = cross_product(sketch, sketch)
    summed = all_reduce(gram_local)
    inverse_low = lower_inverse(summed)
    basis_full = lax.dot_general(
        sketch,
        inverse_low,
        (((1,), (1,)), ((), ())),
        precision=lax.Precision.HIGHEST,
        preferred_element_type=jnp.float32,
    ) * math.sqrt(total_rows)
    basis_half = basis_full.astype(jnp.bfloat16)
    partial = lax.dot_general(
        snapshots, basis_half, (((0,), (0,)), ((), ())), preferred_element_type=jnp.float32
    )
    grid_part = reduce_scatter(partial, "cols", n_cols)
    projected = reduce_scatter(grid_part.T, "rows", n_rows)
    coeffs = projected * (1.0 / math.sqrt(total_rows))
    return (basis_full, coeffs)


def solution(mesh):
    placed = (P(("rows", "cols"), None), P())
    return jax.shard_map(
        body,
        mesh=mesh,
        in_specs=placed,
        out_specs=(P(("rows", "cols"), None), P("rows", "cols")),
        check_vma=False,
    )
```

```python
import functools
import math

import jax
import jax.numpy as jnp
from jax import lax
from jax.experimental import pallas as pl
from jax.experimental.pallas import tpu as pltpu
from jax.sharding import PartitionSpec as P


def cross_product(left, right):
    return lax.dot_general(
        left,
        right,
        (((0,), (0,)), ((), ())),
        precision=lax.Precision.HIGHEST,
        preferred_element_type=jnp.float32,
    )


def matmul(left, right):
    return jnp.dot(left, right, precision=lax.Precision.HIGHEST, preferred_element_type=jnp.float32)


def lower_inverse(gram):
    half = gram.shape[0] // 2
    identity = jnp.eye(half, dtype=gram.dtype)
    low11 = jnp.linalg.cholesky(gram[:half, :half])
    inv11 = lax.linalg.triangular_solve(low11, identity, left_side=True, lower=True)
    low21 = matmul(gram[half:, :half], inv11.T)
    low22 = jnp.linalg.cholesky(gram[half:, half:] - matmul(low21, low21.T))
    inv22 = lax.linalg.triangular_solve(low22, identity, left_side=True, lower=True)
    inv21 = -matmul(inv22, matmul(low21, inv11))
    top = jnp.concatenate([inv11, jnp.zeros_like(inv11)], axis=1)
    return jnp.concatenate([top, jnp.concatenate([inv21, inv22], axis=1)], axis=0)


def reduce_scatter(x, axis, n):
    chunks = x.reshape(n, x.shape[0] // n, *x.shape[1:])
    return lax.all_to_all(chunks, axis, 0, 0, tiled=True).sum(0)


def all_reduce_kernel(n_rows, n_cols, local_ref, out_ref, recv1, part, recv2, total,
                      send1, arrive1, send2, arrive2, send3, arrive3, send4, arrive4):
    me_r = lax.axis_index("rows")
    me_c = lax.axis_index("cols")

    def along(n, mine, step):
        def visit(i, carry):
            step(lax.rem(mine + 1 + i, n))
            return carry

        lax.fori_loop(0, n - 1, visit, 0)

    def copy(src, dst, send, arrive, device):
        return pltpu.make_async_remote_copy(
            src_ref=src, dst_ref=dst, send_sem=send, recv_sem=arrive,
            device_id=device, device_id_type=pl.DeviceIdType.MESH,
        )

    barrier = pltpu.get_barrier_semaphore()
    along(n_cols, me_c, lambda c: pl.semaphore_signal(
        barrier, inc=1, device_id=(me_r, c), device_id_type=pl.DeviceIdType.MESH))
    along(n_rows, me_r, lambda r: pl.semaphore_signal(
        barrier, inc=1, device_id=(r, me_c), device_id_type=pl.DeviceIdType.MESH))
    pl.semaphore_wait(barrier, n_cols + n_rows - 2)

    def scatter1(c):
        return copy(local_ref.at[c], recv1.at[me_c], send1.at[c], arrive1.at[me_c], (me_r, c))

    along(n_cols, me_c, lambda c: scatter1(c).start())
    recv1[me_c] = local_ref[me_c]
    along(n_cols, me_c, lambda c: copy(recv1.at[c], recv1.at[c], send1.at[c], arrive1.at[c], (me_r, c)).wait_recv())
    along(n_cols, me_c, lambda c: scatter1(c).wait_send())
    summed = jnp.sum(recv1[...], axis=0)
    share = part.shape[1]
    for r in range(n_rows):
        part[r] = summed[r * share:(r + 1) * share]

    def scatter2(r):
        return copy(part.at[r], recv2.at[me_r], send2.at[r], arrive2.at[me_r], (r, me_c))

    along(n_rows, me_r, lambda r: scatter2(r).start())
    recv2[me_r] = part[me_r]
    along(n_rows, me_r, lambda r: copy(recv2.at[r], recv2.at[r], send2.at[r], arrive2.at[r], (r, me_c)).wait_recv())
    along(n_rows, me_r, lambda r: scatter2(r).wait_send())
    total[...] = jnp.sum(recv2[...], axis=0)

    def gather3(r):
        return copy(total, out_ref.at[me_c, me_r], send3.at[r], arrive3.at[me_r], (r, me_c))

    along(n_rows, me_r, lambda r: gather3(r).start())
    out_ref[me_c, me_r] = total[...]
    along(n_rows, me_r, lambda r: copy(out_ref.at[me_c, r], out_ref.at[me_c, r], send3.at[r], arrive3.at[r], (r, me_c)).wait_recv())
    along(n_rows, me_r, lambda r: gather3(r).wait_send())

    def gather4(c):
        return copy(out_ref.at[me_c], out_ref.at[me_c], send4.at[c], arrive4.at[me_c], (me_r, c))

    along(n_cols, me_c, lambda c: gather4(c).start())
    along(n_cols, me_c, lambda c: copy(out_ref.at[c], out_ref.at[c], send4.at[c], arrive4.at[c], (me_r, c)).wait_recv())
    along(n_cols, me_c, lambda c: gather4(c).wait_send())


def all_reduce(x):
    n_rows = lax.axis_size("rows")
    n_cols = lax.axis_size("cols")
    rows, width = x.shape
    block = rows // n_cols
    out = pl.pallas_call(
        functools.partial(all_reduce_kernel, n_rows, n_cols),
        out_shape=jax.ShapeDtypeStruct((n_cols, n_rows, block // n_rows, width), x.dtype),
        in_specs=[pl.BlockSpec(memory_space=pltpu.VMEM)],
        out_specs=pl.BlockSpec(memory_space=pltpu.VMEM),
        scratch_shapes=[
            pltpu.VMEM((n_cols, block, width), x.dtype),
            pltpu.VMEM((n_rows, block // n_rows, width), x.dtype),
            pltpu.VMEM((n_rows, block // n_rows, width), x.dtype),
            pltpu.VMEM((block // n_rows, width), x.dtype),
            pltpu.SemaphoreType.DMA((n_cols,)),
            pltpu.SemaphoreType.DMA((n_cols,)),
            pltpu.SemaphoreType.DMA((n_rows,)),
            pltpu.SemaphoreType.DMA((n_rows,)),
            pltpu.SemaphoreType.DMA((n_rows,)),
            pltpu.SemaphoreType.DMA((n_rows,)),
            pltpu.SemaphoreType.DMA((n_cols,)),
            pltpu.SemaphoreType.DMA((n_cols,)),
        ],
        compiler_params=pltpu.CompilerParams(collective_id=0, has_side_effects=True),
    )(x.reshape(n_cols, block, width))
    return out.reshape(rows, width)


def projection_kernel(n_rows, n_cols, local_ref, out_ref, from_core, by_chip, from_chip, part, from_row,
                      send_a, arrive_a, send_b, arrive_b, send_c, arrive_c):
    me_r = lax.axis_index("rows")
    me_c = lax.axis_index("cols")
    core = lax.rem(me_c, 2)
    chip = me_c // 2
    partner = me_c + 1 - 2 * core
    n_chips = n_cols // 2
    width = local_ref.shape[1] // n_cols

    def columns(c):
        return pl.ds(pl.multiple_of(c * width, width), width)

    def copy(src, dst, send, arrive, device):
        return pltpu.make_async_remote_copy(
            src_ref=src, dst_ref=dst, send_sem=send, recv_sem=arrive,
            device_id=device, device_id_type=pl.DeviceIdType.MESH,
        )

    def along(n, mine, step):
        def visit(i, carry):
            step(lax.rem(mine + 1 + i, n))
            return carry

        lax.fori_loop(0, n - 1, visit, 0)

    barrier = pltpu.get_barrier_semaphore()
    signal = functools.partial(pl.semaphore_signal, barrier, 1, device_id_type=pl.DeviceIdType.MESH)
    signal(device_id=(me_r, partner))
    along(n_chips, chip, lambda x: signal(device_id=(me_r, x * 2 + core)))
    along(n_rows, me_r, lambda r: signal(device_id=(r, me_c)))
    pl.semaphore_wait(barrier, n_chips + n_rows - 1)

    def swap(x):
        return copy(local_ref.at[:, columns(x * 2 + 1 - core)], from_core.at[x],
                    send_a.at[x], arrive_a.at[x], (me_r, partner))

    for x in range(n_chips):
        swap(x).start()
    for x in range(n_chips):
        swap(x).wait_recv()
    for x in range(n_chips):
        swap(x).wait_send()
    for x in range(n_chips):
        by_chip[x] = local_ref[:, columns(x * 2 + core)] + from_core[x]

    def share(x):
        return copy(by_chip.at[x], from_chip.at[chip], send_b.at[x], arrive_b.at[chip], (me_r, x * 2 + core))

    along(n_chips, chip, lambda x: share(x).start())
    from_chip[chip] = by_chip[chip]
    along(n_chips, chip, lambda x: copy(from_chip.at[x], from_chip.at[x], send_b.at[x], arrive_b.at[x],
                                        (me_r, x * 2 + core)).wait_recv())
    along(n_chips, chip, lambda x: share(x).wait_send())
    part[...] = jnp.sum(from_chip[...], axis=0).reshape(part.shape)

    def scatter(r):
        return copy(part.at[r], from_row.at[me_r], send_c.at[r], arrive_c.at[me_r], (r, me_c))

    along(n_rows, me_r, lambda r: scatter(r).start())
    from_row[me_r] = part[me_r]
    along(n_rows, me_r, lambda r: copy(from_row.at[r], from_row.at[r], send_c.at[r], arrive_c.at[r],
                                       (r, me_c)).wait_recv())
    along(n_rows, me_r, lambda r: scatter(r).wait_send())
    out_ref[...] = jnp.sum(from_row[...], axis=0)


def reduce_projection(partial):
    n_rows = lax.axis_size("rows")
    n_cols = lax.axis_size("cols")
    rank, grid = partial.shape
    width = grid // n_cols
    share = rank // n_rows
    n_chips = n_cols // 2
    return pl.pallas_call(
        functools.partial(projection_kernel, n_rows, n_cols),
        out_shape=jax.ShapeDtypeStruct((share, width), partial.dtype),
        in_specs=[pl.BlockSpec(memory_space=pltpu.VMEM)],
        out_specs=pl.BlockSpec(memory_space=pltpu.VMEM),
        scratch_shapes=[
            pltpu.VMEM((n_chips, rank, width), partial.dtype),
            pltpu.VMEM((n_chips, rank, width), partial.dtype),
            pltpu.VMEM((n_chips, rank, width), partial.dtype),
            pltpu.VMEM((n_rows, share, width), partial.dtype),
            pltpu.VMEM((n_rows, share, width), partial.dtype),
            pltpu.SemaphoreType.DMA((n_chips,)),
            pltpu.SemaphoreType.DMA((n_chips,)),
            pltpu.SemaphoreType.DMA((n_chips,)),
            pltpu.SemaphoreType.DMA((n_chips,)),
            pltpu.SemaphoreType.DMA((n_rows,)),
            pltpu.SemaphoreType.DMA((n_rows,)),
        ],
        compiler_params=pltpu.CompilerParams(collective_id=1, has_side_effects=True),
    )(partial)


def body(snapshots, test_matrix):
    n_rows = lax.axis_size("rows")
    n_cols = lax.axis_size("cols")
    rows_here = snapshots.shape[0]
    total_rows = rows_here * n_rows * n_cols
    sketch = jnp.dot(snapshots, test_matrix, preferred_element_type=jnp.float32)
    gram_local = cross_product(sketch, sketch)
    summed = all_reduce(gram_local)
    inverse_low = lower_inverse(summed)
    basis_full = lax.dot_general(
        sketch,
        inverse_low,
        (((1,), (1,)), ((), ())),
        precision=lax.Precision.HIGHEST,
        preferred_element_type=jnp.float32,
    ) * math.sqrt(total_rows)
    basis_half = basis_full.astype(jnp.bfloat16)
    partial = lax.dot_general(
        basis_half, snapshots, (((0,), (0,)), ((), ())), preferred_element_type=jnp.float32
    )
    projected = reduce_projection(partial)
    coeffs = projected * (1.0 / math.sqrt(total_rows))
    return (basis_full, coeffs)


def solution(mesh):
    placed = (P(("rows", "cols"), None), P())
    return jax.shard_map(
        body,
        mesh=mesh,
        in_specs=placed,
        out_specs=(P(("rows", "cols"), None), P("rows", "cols")),
        check_vma=False,
    )
```

```python
import functools
import math

import jax
import jax.numpy as jnp
from jax import lax
from jax.experimental import pallas as pl
from jax.experimental.pallas import tpu as pltpu
from jax.sharding import PartitionSpec as P


def cross_product(left, right):
    return lax.dot_general(
        left,
        right,
        (((0,), (0,)), ((), ())),
        precision=lax.Precision.HIGHEST,
        preferred_element_type=jnp.float32,
    )


def matmul(left, right):
    return jnp.dot(left, right, precision=lax.Precision.HIGHEST, preferred_element_type=jnp.float32)


def lower_inverse(gram):
    half = gram.shape[0] // 2
    inv11 = factor_inverse(gram[:half, :half])
    low21 = matmul(gram[half:, :half], inv11.T)
    inv22 = factor_inverse(gram[half:, half:] - matmul(low21, low21.T))
    inv21 = -matmul(inv22, matmul(low21, inv11))
    top = jnp.concatenate([inv11, jnp.zeros_like(inv11)], axis=1)
    return jnp.concatenate([top, jnp.concatenate([inv21, inv22], axis=1)], axis=0)


def reduce_scatter(x, axis, n):
    chunks = x.reshape(n, x.shape[0] // n, *x.shape[1:])
    return lax.all_to_all(chunks, axis, 0, 0, tiled=True).sum(0)


def all_reduce_kernel(n_rows, n_cols, local_ref, out_ref, recv1, part, recv2, total,
                      send1, arrive1, send2, arrive2, send3, arrive3, send4, arrive4):
    me_r = lax.axis_index("rows")
    me_c = lax.axis_index("cols")

    def along(n, mine, step):
        def visit(i, carry):
            step(lax.rem(mine + 1 + i, n))
            return carry

        lax.fori_loop(0, n - 1, visit, 0)

    def copy(src, dst, send, arrive, device):
        return pltpu.make_async_remote_copy(
            src_ref=src, dst_ref=dst, send_sem=send, recv_sem=arrive,
            device_id=device, device_id_type=pl.DeviceIdType.MESH,
        )

    barrier = pltpu.get_barrier_semaphore()
    along(n_cols, me_c, lambda c: pl.semaphore_signal(
        barrier, inc=1, device_id=(me_r, c), device_id_type=pl.DeviceIdType.MESH))
    along(n_rows, me_r, lambda r: pl.semaphore_signal(
        barrier, inc=1, device_id=(r, me_c), device_id_type=pl.DeviceIdType.MESH))
    pl.semaphore_wait(barrier, n_cols + n_rows - 2)

    def scatter1(c):
        return copy(local_ref.at[c], recv1.at[me_c], send1.at[c], arrive1.at[me_c], (me_r, c))

    along(n_cols, me_c, lambda c: scatter1(c).start())
    recv1[me_c] = local_ref[me_c]
    along(n_cols, me_c, lambda c: copy(recv1.at[c], recv1.at[c], send1.at[c], arrive1.at[c], (me_r, c)).wait_recv())
    along(n_cols, me_c, lambda c: scatter1(c).wait_send())
    summed = jnp.sum(recv1[...], axis=0)
    share = part.shape[1]
    for r in range(n_rows):
        part[r] = summed[r * share:(r + 1) * share]

    def scatter2(r):
        return copy(part.at[r], recv2.at[me_r], send2.at[r], arrive2.at[me_r], (r, me_c))

    along(n_rows, me_r, lambda r: scatter2(r).start())
    recv2[me_r] = part[me_r]
    along(n_rows, me_r, lambda r: copy(recv2.at[r], recv2.at[r], send2.at[r], arrive2.at[r], (r, me_c)).wait_recv())
    along(n_rows, me_r, lambda r: scatter2(r).wait_send())
    total[...] = jnp.sum(recv2[...], axis=0)

    def gather3(r):
        return copy(total, out_ref.at[me_c, me_r], send3.at[r], arrive3.at[me_r], (r, me_c))

    along(n_rows, me_r, lambda r: gather3(r).start())
    out_ref[me_c, me_r] = total[...]
    along(n_rows, me_r, lambda r: copy(out_ref.at[me_c, r], out_ref.at[me_c, r], send3.at[r], arrive3.at[r], (r, me_c)).wait_recv())
    along(n_rows, me_r, lambda r: gather3(r).wait_send())

    def gather4(c):
        return copy(out_ref.at[me_c], out_ref.at[me_c], send4.at[c], arrive4.at[me_c], (me_r, c))

    along(n_cols, me_c, lambda c: gather4(c).start())
    along(n_cols, me_c, lambda c: copy(out_ref.at[c], out_ref.at[c], send4.at[c], arrive4.at[c], (me_r, c)).wait_recv())
    along(n_cols, me_c, lambda c: gather4(c).wait_send())


def all_reduce(x):
    n_rows = lax.axis_size("rows")
    n_cols = lax.axis_size("cols")
    rows, width = x.shape
    block = rows // n_cols
    out = pl.pallas_call(
        functools.partial(all_reduce_kernel, n_rows, n_cols),
        out_shape=jax.ShapeDtypeStruct((n_cols, n_rows, block // n_rows, width), x.dtype),
        in_specs=[pl.BlockSpec(memory_space=pltpu.VMEM)],
        out_specs=pl.BlockSpec(memory_space=pltpu.VMEM),
        scratch_shapes=[
            pltpu.VMEM((n_cols, block, width), x.dtype),
            pltpu.VMEM((n_rows, block // n_rows, width), x.dtype),
            pltpu.VMEM((n_rows, block // n_rows, width), x.dtype),
            pltpu.VMEM((block // n_rows, width), x.dtype),
            pltpu.SemaphoreType.DMA((n_cols,)),
            pltpu.SemaphoreType.DMA((n_cols,)),
            pltpu.SemaphoreType.DMA((n_rows,)),
            pltpu.SemaphoreType.DMA((n_rows,)),
            pltpu.SemaphoreType.DMA((n_rows,)),
            pltpu.SemaphoreType.DMA((n_rows,)),
            pltpu.SemaphoreType.DMA((n_cols,)),
            pltpu.SemaphoreType.DMA((n_cols,)),
        ],
        compiler_params=pltpu.CompilerParams(collective_id=0, has_side_effects=True),
    )(x.reshape(n_cols, block, width))
    return out.reshape(rows, width)


def projection_kernel(n_rows, n_cols, local_ref, out_ref, from_core, by_chip, from_chip, part, from_row,
                      send_a, arrive_a, send_b, arrive_b, send_c, arrive_c):
    me_r = lax.axis_index("rows")
    me_c = lax.axis_index("cols")
    core = lax.rem(me_c, 2)
    chip = me_c // 2
    partner = me_c + 1 - 2 * core
    n_chips = n_cols // 2
    width = local_ref.shape[1] // n_cols

    def columns(c):
        return pl.ds(pl.multiple_of(c * width, width), width)

    def copy(src, dst, send, arrive, device):
        return pltpu.make_async_remote_copy(
            src_ref=src, dst_ref=dst, send_sem=send, recv_sem=arrive,
            device_id=device, device_id_type=pl.DeviceIdType.MESH,
        )

    def along(n, mine, step):
        def visit(i, carry):
            step(lax.rem(mine + 1 + i, n))
            return carry

        lax.fori_loop(0, n - 1, visit, 0)

    barrier = pltpu.get_barrier_semaphore()
    signal = functools.partial(pl.semaphore_signal, barrier, 1, device_id_type=pl.DeviceIdType.MESH)
    signal(device_id=(me_r, partner))
    along(n_chips, chip, lambda x: signal(device_id=(me_r, x * 2 + core)))
    along(n_rows, me_r, lambda r: signal(device_id=(r, me_c)))
    pl.semaphore_wait(barrier, n_chips + n_rows - 1)

    def swap(x):
        return copy(local_ref.at[:, columns(x * 2 + 1 - core)], from_core.at[x],
                    send_a.at[x], arrive_a.at[x], (me_r, partner))

    for x in range(n_chips):
        swap(x).start()
    for x in range(n_chips):
        swap(x).wait_recv()
    for x in range(n_chips):
        swap(x).wait_send()
    for x in range(n_chips):
        by_chip[x] = local_ref[:, columns(x * 2 + core)] + from_core[x]

    def share(x):
        return copy(by_chip.at[x], from_chip.at[chip], send_b.at[x], arrive_b.at[chip], (me_r, x * 2 + core))

    along(n_chips, chip, lambda x: share(x).start())
    from_chip[chip] = by_chip[chip]
    along(n_chips, chip, lambda x: copy(from_chip.at[x], from_chip.at[x], send_b.at[x], arrive_b.at[x],
                                        (me_r, x * 2 + core)).wait_recv())
    along(n_chips, chip, lambda x: share(x).wait_send())
    part[...] = jnp.sum(from_chip[...], axis=0).reshape(part.shape)

    def scatter(r):
        return copy(part.at[r], from_row.at[me_r], send_c.at[r], arrive_c.at[me_r], (r, me_c))

    along(n_rows, me_r, lambda r: scatter(r).start())
    from_row[me_r] = part[me_r]
    along(n_rows, me_r, lambda r: copy(from_row.at[r], from_row.at[r], send_c.at[r], arrive_c.at[r],
                                       (r, me_c)).wait_recv())
    along(n_rows, me_r, lambda r: scatter(r).wait_send())
    out_ref[...] = jnp.sum(from_row[...], axis=0)


def reduce_projection(partial):
    n_rows = lax.axis_size("rows")
    n_cols = lax.axis_size("cols")
    rank, grid = partial.shape
    width = grid // n_cols
    share = rank // n_rows
    n_chips = n_cols // 2
    return pl.pallas_call(
        functools.partial(projection_kernel, n_rows, n_cols),
        out_shape=jax.ShapeDtypeStruct((share, width), partial.dtype),
        in_specs=[pl.BlockSpec(memory_space=pltpu.VMEM)],
        out_specs=pl.BlockSpec(memory_space=pltpu.VMEM),
        scratch_shapes=[
            pltpu.VMEM((n_chips, rank, width), partial.dtype),
            pltpu.VMEM((n_chips, rank, width), partial.dtype),
            pltpu.VMEM((n_chips, rank, width), partial.dtype),
            pltpu.VMEM((n_rows, share, width), partial.dtype),
            pltpu.VMEM((n_rows, share, width), partial.dtype),
            pltpu.SemaphoreType.DMA((n_chips,)),
            pltpu.SemaphoreType.DMA((n_chips,)),
            pltpu.SemaphoreType.DMA((n_chips,)),
            pltpu.SemaphoreType.DMA((n_chips,)),
            pltpu.SemaphoreType.DMA((n_rows,)),
            pltpu.SemaphoreType.DMA((n_rows,)),
        ],
        compiler_params=pltpu.CompilerParams(collective_id=1, has_side_effects=True),
    )(partial)


def factor_inverse_kernel(gram_ref, inverse_ref):
    size = gram_ref.shape[0]
    sub = lax.broadcasted_iota(jnp.int32, (size, size), 0)
    lane = lax.broadcasted_iota(jnp.int32, (size, size), 1)
    lane_row = lax.broadcasted_iota(jnp.int32, (1, size), 1)
    sub_col = lax.broadcasted_iota(jnp.int32, (size, 1), 0)

    def step(k, carry):
        work, inverse = carry
        row = jnp.sum(jnp.where(sub == k, work, 0.0), axis=0, keepdims=True)
        column = jnp.sum(jnp.where(lane == k, work, 0.0), axis=1, keepdims=True)
        pivot = jnp.sum(jnp.where(lane_row == k, row, 0.0), axis=1, keepdims=True)
        scale = lax.rsqrt(pivot)
        low_row = jnp.where(lane_row >= k, row * scale, 0.0)
        low_column = jnp.where(sub_col >= k, column * scale, 0.0)
        work = work - low_column * low_row
        inverse_row = jnp.sum(jnp.where(sub == k, inverse, 0.0), axis=0, keepdims=True) * scale
        below = jnp.where(sub_col > k, low_column, 0.0)
        inverse = jnp.where(sub == k, inverse_row, inverse - below * inverse_row)
        return work, inverse

    identity = jnp.where(sub == lane, 1.0, 0.0).astype(jnp.float32)
    _, inverse = lax.fori_loop(0, size, step, (gram_ref[...], identity))
    inverse_ref[...] = inverse


def factor_inverse(gram):
    return pl.pallas_call(
        factor_inverse_kernel,
        out_shape=jax.ShapeDtypeStruct(gram.shape, gram.dtype),
        in_specs=[pl.BlockSpec(memory_space=pltpu.VMEM)],
        out_specs=pl.BlockSpec(memory_space=pltpu.VMEM),
    )(gram)


def body(snapshots, test_matrix):
    n_rows = lax.axis_size("rows")
    n_cols = lax.axis_size("cols")
    rows_here = snapshots.shape[0]
    total_rows = rows_here * n_rows * n_cols
    sketch = jnp.dot(snapshots, test_matrix, preferred_element_type=jnp.float32)
    gram_local = cross_product(sketch, sketch)
    summed = all_reduce(gram_local)
    inverse_low = lower_inverse(summed)
    basis_full = lax.dot_general(
        sketch,
        inverse_low,
        (((1,), (1,)), ((), ())),
        precision=lax.Precision.HIGHEST,
        preferred_element_type=jnp.float32,
    ) * math.sqrt(total_rows)
    basis_half = basis_full.astype(jnp.bfloat16)
    partial = lax.dot_general(
        basis_half, snapshots, (((0,), (0,)), ((), ())), preferred_element_type=jnp.float32
    )
    projected = reduce_projection(partial)
    coeffs = projected * (1.0 / math.sqrt(total_rows))
    return (basis_full, coeffs)


def solution(mesh):
    placed = (P(("rows", "cols"), None), P())
    return jax.shard_map(
        body,
        mesh=mesh,
        in_specs=placed,
        out_specs=(P(("rows", "cols"), None), P("rows", "cols")),
        check_vma=False,
    )
```

```python
import functools
import math

import jax
import jax.numpy as jnp
from jax import lax
from jax.experimental import pallas as pl
from jax.experimental.pallas import tpu as pltpu
from jax.sharding import PartitionSpec as P


def cross_product(left, right):
    return lax.dot_general(
        left,
        right,
        (((0,), (0,)), ((), ())),
        precision=lax.Precision.HIGHEST,
        preferred_element_type=jnp.float32,
    )


def matmul(left, right):
    return jnp.dot(left, right, precision=lax.Precision.HIGHEST, preferred_element_type=jnp.float32)


def lower_inverse(gram):
    half = gram.shape[0] // 2
    inv11 = factor_inverse(gram[:half, :half])
    low21 = matmul(gram[half:, :half], inv11.T)
    inv22 = factor_inverse(gram[half:, half:] - matmul(low21, low21.T))
    inv21 = -matmul(inv22, matmul(low21, inv11))
    top = jnp.concatenate([inv11, jnp.zeros_like(inv11)], axis=1)
    return jnp.concatenate([top, jnp.concatenate([inv21, inv22], axis=1)], axis=0)


def reduce_scatter(x, axis, n):
    chunks = x.reshape(n, x.shape[0] // n, *x.shape[1:])
    return lax.all_to_all(chunks, axis, 0, 0, tiled=True).sum(0)


def all_reduce_kernel(n_rows, n_cols, local_ref, out_ref, recv1, part, recv2, total,
                      send1, arrive1, send2, arrive2, send3, arrive3, send4, arrive4):
    me_r = lax.axis_index("rows")
    me_c = lax.axis_index("cols")

    def along(n, mine, step):
        def visit(i, carry):
            step(lax.rem(mine + 1 + i, n))
            return carry

        lax.fori_loop(0, n - 1, visit, 0)

    def copy(src, dst, send, arrive, device):
        return pltpu.make_async_remote_copy(
            src_ref=src, dst_ref=dst, send_sem=send, recv_sem=arrive,
            device_id=device, device_id_type=pl.DeviceIdType.MESH,
        )

    barrier = pltpu.get_barrier_semaphore()
    along(n_cols, me_c, lambda c: pl.semaphore_signal(
        barrier, inc=1, device_id=(me_r, c), device_id_type=pl.DeviceIdType.MESH))
    along(n_rows, me_r, lambda r: pl.semaphore_signal(
        barrier, inc=1, device_id=(r, me_c), device_id_type=pl.DeviceIdType.MESH))
    pl.semaphore_wait(barrier, n_cols + n_rows - 2)

    def scatter1(c):
        return copy(local_ref.at[c], recv1.at[me_c], send1.at[c], arrive1.at[me_c], (me_r, c))

    along(n_cols, me_c, lambda c: scatter1(c).start())
    recv1[me_c] = local_ref[me_c]
    along(n_cols, me_c, lambda c: copy(recv1.at[c], recv1.at[c], send1.at[c], arrive1.at[c], (me_r, c)).wait_recv())
    along(n_cols, me_c, lambda c: scatter1(c).wait_send())
    summed = jnp.sum(recv1[...], axis=0)
    share = part.shape[1]
    for r in range(n_rows):
        part[r] = summed[r * share:(r + 1) * share]

    def scatter2(r):
        return copy(part.at[r], recv2.at[me_r], send2.at[r], arrive2.at[me_r], (r, me_c))

    along(n_rows, me_r, lambda r: scatter2(r).start())
    recv2[me_r] = part[me_r]
    along(n_rows, me_r, lambda r: copy(recv2.at[r], recv2.at[r], send2.at[r], arrive2.at[r], (r, me_c)).wait_recv())
    along(n_rows, me_r, lambda r: scatter2(r).wait_send())
    total[...] = jnp.sum(recv2[...], axis=0)

    def gather3(r):
        return copy(total, out_ref.at[me_c, me_r], send3.at[r], arrive3.at[me_r], (r, me_c))

    along(n_rows, me_r, lambda r: gather3(r).start())
    out_ref[me_c, me_r] = total[...]
    along(n_rows, me_r, lambda r: copy(out_ref.at[me_c, r], out_ref.at[me_c, r], send3.at[r], arrive3.at[r], (r, me_c)).wait_recv())
    along(n_rows, me_r, lambda r: gather3(r).wait_send())

    def gather4(c):
        return copy(out_ref.at[me_c], out_ref.at[me_c], send4.at[c], arrive4.at[me_c], (me_r, c))

    along(n_cols, me_c, lambda c: gather4(c).start())
    along(n_cols, me_c, lambda c: copy(out_ref.at[c], out_ref.at[c], send4.at[c], arrive4.at[c], (me_r, c)).wait_recv())
    along(n_cols, me_c, lambda c: gather4(c).wait_send())


def all_reduce(x):
    n_rows = lax.axis_size("rows")
    n_cols = lax.axis_size("cols")
    rows, width = x.shape
    block = rows // n_cols
    out = pl.pallas_call(
        functools.partial(all_reduce_kernel, n_rows, n_cols),
        out_shape=jax.ShapeDtypeStruct((n_cols, n_rows, block // n_rows, width), x.dtype),
        in_specs=[pl.BlockSpec(memory_space=pltpu.VMEM)],
        out_specs=pl.BlockSpec(memory_space=pltpu.VMEM),
        scratch_shapes=[
            pltpu.VMEM((n_cols, block, width), x.dtype),
            pltpu.VMEM((n_rows, block // n_rows, width), x.dtype),
            pltpu.VMEM((n_rows, block // n_rows, width), x.dtype),
            pltpu.VMEM((block // n_rows, width), x.dtype),
            pltpu.SemaphoreType.DMA((n_cols,)),
            pltpu.SemaphoreType.DMA((n_cols,)),
            pltpu.SemaphoreType.DMA((n_rows,)),
            pltpu.SemaphoreType.DMA((n_rows,)),
            pltpu.SemaphoreType.DMA((n_rows,)),
            pltpu.SemaphoreType.DMA((n_rows,)),
            pltpu.SemaphoreType.DMA((n_cols,)),
            pltpu.SemaphoreType.DMA((n_cols,)),
        ],
        compiler_params=pltpu.CompilerParams(collective_id=0, has_side_effects=True),
    )(x.reshape(n_cols, block, width))
    return out.reshape(rows, width)


def projection_kernel(n_rows, n_cols, local_ref, out_ref, from_core, by_chip, from_chip, part, from_row,
                      send_a, arrive_a, send_b, arrive_b, send_c, arrive_c):
    me_r = lax.axis_index("rows")
    me_c = lax.axis_index("cols")
    core = lax.rem(me_c, 2)
    chip = me_c // 2
    partner = me_c + 1 - 2 * core
    n_chips = n_cols // 2
    width = local_ref.shape[1] // n_cols

    def columns(c):
        return pl.ds(pl.multiple_of(c * width, width), width)

    def copy(src, dst, send, arrive, device):
        return pltpu.make_async_remote_copy(
            src_ref=src, dst_ref=dst, send_sem=send, recv_sem=arrive,
            device_id=device, device_id_type=pl.DeviceIdType.MESH,
        )

    def along(n, mine, step):
        def visit(i, carry):
            step(lax.rem(mine + 1 + i, n))
            return carry

        lax.fori_loop(0, n - 1, visit, 0)

    barrier = pltpu.get_barrier_semaphore()
    signal = functools.partial(pl.semaphore_signal, barrier, 1, device_id_type=pl.DeviceIdType.MESH)
    signal(device_id=(me_r, partner))
    along(n_chips, chip, lambda x: signal(device_id=(me_r, x * 2 + core)))
    along(n_rows, me_r, lambda r: signal(device_id=(r, me_c)))
    pl.semaphore_wait(barrier, n_chips + n_rows - 1)

    def swap(x):
        return copy(local_ref.at[:, columns(x * 2 + 1 - core)], from_core.at[x],
                    send_a.at[x], arrive_a.at[x], (me_r, partner))

    for x in range(n_chips):
        swap(x).start()
    for x in range(n_chips):
        swap(x).wait_recv()
    for x in range(n_chips):
        swap(x).wait_send()
    for x in range(n_chips):
        by_chip[x] = local_ref[:, columns(x * 2 + core)] + from_core[x]

    def share(x):
        return copy(by_chip.at[x], from_chip.at[chip], send_b.at[x], arrive_b.at[chip], (me_r, x * 2 + core))

    along(n_chips, chip, lambda x: share(x).start())
    from_chip[chip] = by_chip[chip]
    along(n_chips, chip, lambda x: copy(from_chip.at[x], from_chip.at[x], send_b.at[x], arrive_b.at[x],
                                        (me_r, x * 2 + core)).wait_recv())
    along(n_chips, chip, lambda x: share(x).wait_send())
    part[...] = jnp.sum(from_chip[...], axis=0).reshape(part.shape)

    def scatter(r):
        return copy(part.at[r], from_row.at[me_r], send_c.at[r], arrive_c.at[me_r], (r, me_c))

    along(n_rows, me_r, lambda r: scatter(r).start())
    from_row[me_r] = part[me_r]
    along(n_rows, me_r, lambda r: copy(from_row.at[r], from_row.at[r], send_c.at[r], arrive_c.at[r],
                                       (r, me_c)).wait_recv())
    along(n_rows, me_r, lambda r: scatter(r).wait_send())
    out_ref[...] = jnp.sum(from_row[...], axis=0)


def reduce_projection(partial):
    n_rows = lax.axis_size("rows")
    n_cols = lax.axis_size("cols")
    rank, grid = partial.shape
    width = grid // n_cols
    share = rank // n_rows
    n_chips = n_cols // 2
    return pl.pallas_call(
        functools.partial(projection_kernel, n_rows, n_cols),
        out_shape=jax.ShapeDtypeStruct((share, width), partial.dtype),
        in_specs=[pl.BlockSpec(memory_space=pltpu.VMEM)],
        out_specs=pl.BlockSpec(memory_space=pltpu.VMEM),
        scratch_shapes=[
            pltpu.VMEM((n_chips, rank, width), partial.dtype),
            pltpu.VMEM((n_chips, rank, width), partial.dtype),
            pltpu.VMEM((n_chips, rank, width), partial.dtype),
            pltpu.VMEM((n_rows, share, width), partial.dtype),
            pltpu.VMEM((n_rows, share, width), partial.dtype),
            pltpu.SemaphoreType.DMA((n_chips,)),
            pltpu.SemaphoreType.DMA((n_chips,)),
            pltpu.SemaphoreType.DMA((n_chips,)),
            pltpu.SemaphoreType.DMA((n_chips,)),
            pltpu.SemaphoreType.DMA((n_rows,)),
            pltpu.SemaphoreType.DMA((n_rows,)),
        ],
        compiler_params=pltpu.CompilerParams(collective_id=1, has_side_effects=True),
    )(partial)


def factor_inverse_kernel(gram_ref, inverse_ref, work_ref):
    size = gram_ref.shape[0]
    sub = lax.broadcasted_iota(jnp.int32, (size, size), 0)
    lane = lax.broadcasted_iota(jnp.int32, (size, size), 1)
    lane_row = lax.broadcasted_iota(jnp.int32, (1, size), 1)
    sub_col = lax.broadcasted_iota(jnp.int32, (size, 1), 0)

    def step(k, carry):
        row = work_ref[pl.ds(k, 1), :]
        work = work_ref[...]
        column = jnp.sum(jnp.where(lane == k, work, 0.0), axis=1, keepdims=True)
        pivot = jnp.sum(jnp.where(lane_row == k, row, 0.0), axis=1, keepdims=True)
        scale = lax.rsqrt(pivot)
        low_row = jnp.where(lane_row >= k, row * scale, 0.0)
        low_column = jnp.where(sub_col >= k, column * scale, 0.0)
        work_ref[...] = work - low_column * low_row
        inverse_row = inverse_ref[pl.ds(k, 1), :] * scale
        below = jnp.where(sub_col > k, low_column, 0.0)
        inverse = inverse_ref[...]
        inverse_ref[...] = jnp.where(sub == k, inverse_row, inverse - below * inverse_row)
        return carry

    work_ref[...] = gram_ref[...]
    inverse_ref[...] = jnp.where(sub == lane, 1.0, 0.0).astype(jnp.float32)
    lax.fori_loop(0, size, step, 0)


def factor_inverse(gram):
    return pl.pallas_call(
        factor_inverse_kernel,
        out_shape=jax.ShapeDtypeStruct(gram.shape, gram.dtype),
        in_specs=[pl.BlockSpec(memory_space=pltpu.VMEM)],
        out_specs=pl.BlockSpec(memory_space=pltpu.VMEM),
        scratch_shapes=[pltpu.VMEM(gram.shape, gram.dtype)],
    )(gram)


def body(snapshots, test_matrix):
    n_rows = lax.axis_size("rows")
    n_cols = lax.axis_size("cols")
    rows_here = snapshots.shape[0]
    total_rows = rows_here * n_rows * n_cols
    sketch = jnp.dot(snapshots, test_matrix, preferred_element_type=jnp.float32)
    gram_local = cross_product(sketch, sketch)
    summed = all_reduce(gram_local)
    inverse_low = lower_inverse(summed)
    basis_full = lax.dot_general(
        sketch,
        inverse_low,
        (((1,), (1,)), ((), ())),
        precision=lax.Precision.HIGHEST,
        preferred_element_type=jnp.float32,
    ) * math.sqrt(total_rows)
    basis_half = basis_full.astype(jnp.bfloat16)
    partial = lax.dot_general(
        basis_half, snapshots, (((0,), (0,)), ((), ())), preferred_element_type=jnp.float32
    )
    projected = reduce_projection(partial)
    coeffs = projected * (1.0 / math.sqrt(total_rows))
    return (basis_full, coeffs)


def solution(mesh):
    placed = (P(("rows", "cols"), None), P())
    return jax.shard_map(
        body,
        mesh=mesh,
        in_specs=placed,
        out_specs=(P(("rows", "cols"), None), P("rows", "cols")),
        check_vma=False,
    )
```

```python
import functools
import math

import jax
import jax.numpy as jnp
from jax import lax
from jax.experimental import pallas as pl
from jax.experimental.pallas import tpu as pltpu
from jax.sharding import PartitionSpec as P


def cross_product(left, right):
    return lax.dot_general(
        left,
        right,
        (((0,), (0,)), ((), ())),
        precision=lax.Precision.HIGHEST,
        preferred_element_type=jnp.float32,
    )


def matmul(left, right):
    return jnp.dot(left, right, precision=lax.Precision.HIGHEST, preferred_element_type=jnp.float32)


def reduce_scatter(x, axis, n):
    chunks = x.reshape(n, x.shape[0] // n, *x.shape[1:])
    return lax.all_to_all(chunks, axis, 0, 0, tiled=True).sum(0)


def all_reduce_kernel(n_rows, n_cols, local_ref, out_ref, recv1, part, recv2, total,
                      send1, arrive1, send2, arrive2, send3, arrive3, send4, arrive4):
    me_r = lax.axis_index("rows")
    me_c = lax.axis_index("cols")

    def along(n, mine, step):
        def visit(i, carry):
            step(lax.rem(mine + 1 + i, n))
            return carry

        lax.fori_loop(0, n - 1, visit, 0)

    def copy(src, dst, send, arrive, device):
        return pltpu.make_async_remote_copy(
            src_ref=src, dst_ref=dst, send_sem=send, recv_sem=arrive,
            device_id=device, device_id_type=pl.DeviceIdType.MESH,
        )

    barrier = pltpu.get_barrier_semaphore()
    along(n_cols, me_c, lambda c: pl.semaphore_signal(
        barrier, inc=1, device_id=(me_r, c), device_id_type=pl.DeviceIdType.MESH))
    along(n_rows, me_r, lambda r: pl.semaphore_signal(
        barrier, inc=1, device_id=(r, me_c), device_id_type=pl.DeviceIdType.MESH))
    pl.semaphore_wait(barrier, n_cols + n_rows - 2)

    def scatter1(c):
        return copy(local_ref.at[c], recv1.at[me_c], send1.at[c], arrive1.at[me_c], (me_r, c))

    along(n_cols, me_c, lambda c: scatter1(c).start())
    recv1[me_c] = local_ref[me_c]
    along(n_cols, me_c, lambda c: copy(recv1.at[c], recv1.at[c], send1.at[c], arrive1.at[c], (me_r, c)).wait_recv())
    along(n_cols, me_c, lambda c: scatter1(c).wait_send())
    summed = jnp.sum(recv1[...], axis=0)
    share = part.shape[1]
    for r in range(n_rows):
        part[r] = summed[r * share:(r + 1) * share]

    def scatter2(r):
        return copy(part.at[r], recv2.at[me_r], send2.at[r], arrive2.at[me_r], (r, me_c))

    along(n_rows, me_r, lambda r: scatter2(r).start())
    recv2[me_r] = part[me_r]
    along(n_rows, me_r, lambda r: copy(recv2.at[r], recv2.at[r], send2.at[r], arrive2.at[r], (r, me_c)).wait_recv())
    along(n_rows, me_r, lambda r: scatter2(r).wait_send())
    total[...] = jnp.sum(recv2[...], axis=0)

    def gather3(r):
        return copy(total, out_ref.at[me_c, me_r], send3.at[r], arrive3.at[me_r], (r, me_c))

    along(n_rows, me_r, lambda r: gather3(r).start())
    out_ref[me_c, me_r] = total[...]
    along(n_rows, me_r, lambda r: copy(out_ref.at[me_c, r], out_ref.at[me_c, r], send3.at[r], arrive3.at[r], (r, me_c)).wait_recv())
    along(n_rows, me_r, lambda r: gather3(r).wait_send())

    def gather4(c):
        return copy(out_ref.at[me_c], out_ref.at[me_c], send4.at[c], arrive4.at[me_c], (me_r, c))

    along(n_cols, me_c, lambda c: gather4(c).start())
    along(n_cols, me_c, lambda c: copy(out_ref.at[c], out_ref.at[c], send4.at[c], arrive4.at[c], (me_r, c)).wait_recv())
    along(n_cols, me_c, lambda c: gather4(c).wait_send())


def all_reduce(x):
    n_rows = lax.axis_size("rows")
    n_cols = lax.axis_size("cols")
    rows, width = x.shape
    block = rows // n_cols
    out = pl.pallas_call(
        functools.partial(all_reduce_kernel, n_rows, n_cols),
        out_shape=jax.ShapeDtypeStruct((n_cols, n_rows, block // n_rows, width), x.dtype),
        in_specs=[pl.BlockSpec(memory_space=pltpu.VMEM)],
        out_specs=pl.BlockSpec(memory_space=pltpu.VMEM),
        scratch_shapes=[
            pltpu.VMEM((n_cols, block, width), x.dtype),
            pltpu.VMEM((n_rows, block // n_rows, width), x.dtype),
            pltpu.VMEM((n_rows, block // n_rows, width), x.dtype),
            pltpu.VMEM((block // n_rows, width), x.dtype),
            pltpu.SemaphoreType.DMA((n_cols,)),
            pltpu.SemaphoreType.DMA((n_cols,)),
            pltpu.SemaphoreType.DMA((n_rows,)),
            pltpu.SemaphoreType.DMA((n_rows,)),
            pltpu.SemaphoreType.DMA((n_rows,)),
            pltpu.SemaphoreType.DMA((n_rows,)),
            pltpu.SemaphoreType.DMA((n_cols,)),
            pltpu.SemaphoreType.DMA((n_cols,)),
        ],
        compiler_params=pltpu.CompilerParams(collective_id=0, has_side_effects=True),
    )(x.reshape(n_cols, block, width))
    return out.reshape(rows, width)


def projection_kernel(n_rows, n_cols, local_ref, out_ref, from_core, by_chip, from_chip, part, from_row,
                      send_a, arrive_a, send_b, arrive_b, send_c, arrive_c):
    me_r = lax.axis_index("rows")
    me_c = lax.axis_index("cols")
    core = lax.rem(me_c, 2)
    chip = me_c // 2
    partner = me_c + 1 - 2 * core
    n_chips = n_cols // 2
    width = local_ref.shape[1] // n_cols

    def columns(c):
        return pl.ds(pl.multiple_of(c * width, width), width)

    def copy(src, dst, send, arrive, device):
        return pltpu.make_async_remote_copy(
            src_ref=src, dst_ref=dst, send_sem=send, recv_sem=arrive,
            device_id=device, device_id_type=pl.DeviceIdType.MESH,
        )

    def along(n, mine, step):
        def visit(i, carry):
            step(lax.rem(mine + 1 + i, n))
            return carry

        lax.fori_loop(0, n - 1, visit, 0)

    barrier = pltpu.get_barrier_semaphore()
    signal = functools.partial(pl.semaphore_signal, barrier, 1, device_id_type=pl.DeviceIdType.MESH)
    signal(device_id=(me_r, partner))
    along(n_chips, chip, lambda x: signal(device_id=(me_r, x * 2 + core)))
    along(n_rows, me_r, lambda r: signal(device_id=(r, me_c)))
    pl.semaphore_wait(barrier, n_chips + n_rows - 1)

    def swap(x):
        return copy(local_ref.at[:, columns(x * 2 + 1 - core)], from_core.at[x],
                    send_a.at[x], arrive_a.at[x], (me_r, partner))

    for x in range(n_chips):
        swap(x).start()
    for x in range(n_chips):
        swap(x).wait_recv()
    for x in range(n_chips):
        swap(x).wait_send()
    for x in range(n_chips):
        by_chip[x] = local_ref[:, columns(x * 2 + core)] + from_core[x]

    def share(x):
        return copy(by_chip.at[x], from_chip.at[chip], send_b.at[x], arrive_b.at[chip], (me_r, x * 2 + core))

    along(n_chips, chip, lambda x: share(x).start())
    from_chip[chip] = by_chip[chip]
    along(n_chips, chip, lambda x: copy(from_chip.at[x], from_chip.at[x], send_b.at[x], arrive_b.at[x],
                                        (me_r, x * 2 + core)).wait_recv())
    along(n_chips, chip, lambda x: share(x).wait_send())
    part[...] = jnp.sum(from_chip[...], axis=0).reshape(part.shape)

    def scatter(r):
        return copy(part.at[r], from_row.at[me_r], send_c.at[r], arrive_c.at[me_r], (r, me_c))

    along(n_rows, me_r, lambda r: scatter(r).start())
    from_row[me_r] = part[me_r]
    along(n_rows, me_r, lambda r: copy(from_row.at[r], from_row.at[r], send_c.at[r], arrive_c.at[r],
                                       (r, me_c)).wait_recv())
    along(n_rows, me_r, lambda r: scatter(r).wait_send())
    out_ref[...] = jnp.sum(from_row[...], axis=0)


def reduce_projection(partial):
    n_rows = lax.axis_size("rows")
    n_cols = lax.axis_size("cols")
    rank, grid = partial.shape
    width = grid // n_cols
    share = rank // n_rows
    n_chips = n_cols // 2
    return pl.pallas_call(
        functools.partial(projection_kernel, n_rows, n_cols),
        out_shape=jax.ShapeDtypeStruct((share, width), partial.dtype),
        in_specs=[pl.BlockSpec(memory_space=pltpu.VMEM)],
        out_specs=pl.BlockSpec(memory_space=pltpu.VMEM),
        scratch_shapes=[
            pltpu.VMEM((n_chips, rank, width), partial.dtype),
            pltpu.VMEM((n_chips, rank, width), partial.dtype),
            pltpu.VMEM((n_chips, rank, width), partial.dtype),
            pltpu.VMEM((n_rows, share, width), partial.dtype),
            pltpu.VMEM((n_rows, share, width), partial.dtype),
            pltpu.SemaphoreType.DMA((n_chips,)),
            pltpu.SemaphoreType.DMA((n_chips,)),
            pltpu.SemaphoreType.DMA((n_chips,)),
            pltpu.SemaphoreType.DMA((n_chips,)),
            pltpu.SemaphoreType.DMA((n_rows,)),
            pltpu.SemaphoreType.DMA((n_rows,)),
        ],
        compiler_params=pltpu.CompilerParams(collective_id=1, has_side_effects=True),
    )(partial)


def factor_inverse_block(gram, inverse_ref, work_ref):
    size = gram.shape[0]
    sub = lax.broadcasted_iota(jnp.int32, (size, size), 0)
    lane = lax.broadcasted_iota(jnp.int32, (size, size), 1)
    lane_row = lax.broadcasted_iota(jnp.int32, (1, size), 1)
    sub_col = lax.broadcasted_iota(jnp.int32, (size, 1), 0)

    def step(k, carry):
        row = work_ref[pl.ds(k, 1), :]
        work = work_ref[...]
        column = jnp.sum(jnp.where(lane == k, work, 0.0), axis=1, keepdims=True)
        pivot = jnp.sum(jnp.where(lane_row == k, row, 0.0), axis=1, keepdims=True)
        scale = lax.rsqrt(pivot)
        low_row = jnp.where(lane_row >= k, row * scale, 0.0)
        low_column = jnp.where(sub_col >= k, column * scale, 0.0)
        work_ref[...] = work - low_column * low_row
        inverse_row = inverse_ref[pl.ds(k, 1), :] * scale
        below = jnp.where(sub_col > k, low_column, 0.0)
        inverse = inverse_ref[...]
        inverse_ref[...] = jnp.where(sub == k, inverse_row, inverse - below * inverse_row)
        return carry

    work_ref[...] = gram
    inverse_ref[...] = jnp.where(sub == lane, 1.0, 0.0).astype(jnp.float32)
    lax.fori_loop(0, size, step, 0)


def nt(left, right):
    return lax.dot_general(
        left, right, (((1,), (1,)), ((), ())),
        precision=lax.Precision.HIGHEST, preferred_element_type=jnp.float32,
    )


def lower_inverse_kernel(gram_ref, out_ref, first, second, work_ref):
    half = gram_ref.shape[0] // 2
    factor_inverse_block(gram_ref[:half, :half], first, work_ref)
    inv11 = first[...]
    low21 = nt(gram_ref[half:, :half], inv11)
    factor_inverse_block(gram_ref[half:, half:] - nt(low21, low21), second, work_ref)
    inv22 = second[...]
    out_ref[:half, :half] = inv11
    out_ref[:half, half:] = jnp.zeros_like(inv11)
    out_ref[half:, :half] = -matmul(inv22, matmul(low21, inv11))
    out_ref[half:, half:] = inv22


def lower_inverse(gram):
    half = gram.shape[0] // 2
    block = pltpu.VMEM((half, half), gram.dtype)
    return pl.pallas_call(
        lower_inverse_kernel,
        out_shape=jax.ShapeDtypeStruct(gram.shape, gram.dtype),
        in_specs=[pl.BlockSpec(memory_space=pltpu.VMEM)],
        out_specs=pl.BlockSpec(memory_space=pltpu.VMEM),
        scratch_shapes=[block, block, block],
    )(gram)


def body(snapshots, test_matrix):
    n_rows = lax.axis_size("rows")
    n_cols = lax.axis_size("cols")
    rows_here = snapshots.shape[0]
    total_rows = rows_here * n_rows * n_cols
    sketch = jnp.dot(snapshots, test_matrix, preferred_element_type=jnp.float32)
    gram_local = cross_product(sketch, sketch)
    summed = all_reduce(gram_local)
    inverse_low = lower_inverse(summed)
    basis_full = lax.dot_general(
        sketch,
        inverse_low,
        (((1,), (1,)), ((), ())),
        precision=lax.Precision.HIGHEST,
        preferred_element_type=jnp.float32,
    ) * math.sqrt(total_rows)
    basis_half = basis_full.astype(jnp.bfloat16)
    partial = lax.dot_general(
        basis_half, snapshots, (((0,), (0,)), ((), ())), preferred_element_type=jnp.float32
    )
    projected = reduce_projection(partial)
    coeffs = projected * (1.0 / math.sqrt(total_rows))
    return (basis_full, coeffs)


def solution(mesh):
    placed = (P(("rows", "cols"), None), P())
    return jax.shard_map(
        body,
        mesh=mesh,
        in_specs=placed,
        out_specs=(P(("rows", "cols"), None), P("rows", "cols")),
        check_vma=False,
    )
```

```python
import functools
import math

import jax
import jax.numpy as jnp
from jax import lax
from jax.experimental import pallas as pl
from jax.experimental.pallas import tpu as pltpu
from jax.sharding import PartitionSpec as P


def cross_product(left, right):
    return lax.dot_general(
        left,
        right,
        (((0,), (0,)), ((), ())),
        precision=lax.Precision.HIGHEST,
        preferred_element_type=jnp.float32,
    )


def matmul(left, right):
    return jnp.dot(left, right, precision=lax.Precision.HIGHEST, preferred_element_type=jnp.float32)


def reduce_scatter(x, axis, n):
    chunks = x.reshape(n, x.shape[0] // n, *x.shape[1:])
    return lax.all_to_all(chunks, axis, 0, 0, tiled=True).sum(0)


def all_reduce_kernel(n_rows, n_cols, local_ref, out_ref, recv1, part, recv2, total, rows_in,
                      send1, arrive1, send2, arrive2, send3, arrive3, send4, arrive4):
    me_r = lax.axis_index("rows")
    me_c = lax.axis_index("cols")

    def along(n, mine, step):
        def visit(i, carry):
            step(lax.rem(mine + 1 + i, n))
            return carry

        lax.fori_loop(0, n - 1, visit, 0)

    def copy(src, dst, send, arrive, device):
        return pltpu.make_async_remote_copy(
            src_ref=src, dst_ref=dst, send_sem=send, recv_sem=arrive,
            device_id=device, device_id_type=pl.DeviceIdType.MESH,
        )

    barrier = pltpu.get_barrier_semaphore()
    along(n_cols, me_c, lambda c: pl.semaphore_signal(
        barrier, inc=1, device_id=(me_r, c), device_id_type=pl.DeviceIdType.MESH))
    along(n_rows, me_r, lambda r: pl.semaphore_signal(
        barrier, inc=1, device_id=(r, me_c), device_id_type=pl.DeviceIdType.MESH))
    pl.semaphore_wait(barrier, n_cols + n_rows - 2)

    def scatter1(c):
        return copy(local_ref.at[c], recv1.at[me_c], send1.at[c], arrive1.at[me_c], (me_r, c))

    along(n_cols, me_c, lambda c: scatter1(c).start())
    recv1[me_c] = local_ref[me_c]
    along(n_cols, me_c, lambda c: copy(recv1.at[c], recv1.at[c], send1.at[c], arrive1.at[c], (me_r, c)).wait_recv())
    along(n_cols, me_c, lambda c: scatter1(c).wait_send())
    summed = jnp.sum(recv1[...], axis=0)
    share = part.shape[1]
    for r in range(n_rows):
        part[r] = summed[r * share:(r + 1) * share]

    def scatter2(r):
        return copy(part.at[r], recv2.at[me_r], send2.at[r], arrive2.at[me_r], (r, me_c))

    along(n_rows, me_r, lambda r: scatter2(r).start())
    recv2[me_r] = part[me_r]
    along(n_rows, me_r, lambda r: copy(recv2.at[r], recv2.at[r], send2.at[r], arrive2.at[r], (r, me_c)).wait_recv())
    along(n_rows, me_r, lambda r: scatter2(r).wait_send())
    total[...] = jnp.sum(recv2[...], axis=0)

    def gather3(r):
        return copy(total, rows_in.at[me_r], send3.at[r], arrive3.at[me_r], (r, me_c))

    along(n_rows, me_r, lambda r: gather3(r).start())
    rows_in[me_r] = total[...]
    along(n_rows, me_r, lambda r: copy(rows_in.at[r], rows_in.at[r], send3.at[r], arrive3.at[r], (r, me_c)).wait_recv())
    along(n_rows, me_r, lambda r: gather3(r).wait_send())
    block = n_rows * share

    def rows_of(c):
        return pl.ds(pl.multiple_of(c * block, block), block)

    out_ref[rows_of(me_c), :] = jnp.concatenate([rows_in[r] for r in range(n_rows)], axis=0)

    def gather4(c):
        return copy(out_ref.at[rows_of(me_c)], out_ref.at[rows_of(me_c)], send4.at[c], arrive4.at[me_c], (me_r, c))

    along(n_cols, me_c, lambda c: gather4(c).start())
    along(n_cols, me_c, lambda c: copy(out_ref.at[rows_of(c)], out_ref.at[rows_of(c)], send4.at[c], arrive4.at[c], (me_r, c)).wait_recv())
    along(n_cols, me_c, lambda c: gather4(c).wait_send())


def all_reduce(x):
    n_rows = lax.axis_size("rows")
    n_cols = lax.axis_size("cols")
    rows, width = x.shape
    block = rows // n_cols
    out = pl.pallas_call(
        functools.partial(all_reduce_kernel, n_rows, n_cols),
        out_shape=jax.ShapeDtypeStruct((rows, width), x.dtype),
        in_specs=[pl.BlockSpec(memory_space=pltpu.VMEM)],
        out_specs=pl.BlockSpec(memory_space=pltpu.VMEM),
        scratch_shapes=[
            pltpu.VMEM((n_cols, block, width), x.dtype),
            pltpu.VMEM((n_rows, block // n_rows, width), x.dtype),
            pltpu.VMEM((n_rows, block // n_rows, width), x.dtype),
            pltpu.VMEM((block // n_rows, width), x.dtype),
            pltpu.VMEM((n_rows, block // n_rows, width), x.dtype),
            pltpu.SemaphoreType.DMA((n_cols,)),
            pltpu.SemaphoreType.DMA((n_cols,)),
            pltpu.SemaphoreType.DMA((n_rows,)),
            pltpu.SemaphoreType.DMA((n_rows,)),
            pltpu.SemaphoreType.DMA((n_rows,)),
            pltpu.SemaphoreType.DMA((n_rows,)),
            pltpu.SemaphoreType.DMA((n_cols,)),
            pltpu.SemaphoreType.DMA((n_cols,)),
        ],
        compiler_params=pltpu.CompilerParams(collective_id=0, has_side_effects=True),
    )(x.reshape(n_cols, block, width))
    return out


def projection_kernel(n_rows, n_cols, local_ref, out_ref, from_core, by_chip, from_chip, part, from_row,
                      send_a, arrive_a, send_b, arrive_b, send_c, arrive_c):
    me_r = lax.axis_index("rows")
    me_c = lax.axis_index("cols")
    core = lax.rem(me_c, 2)
    chip = me_c // 2
    partner = me_c + 1 - 2 * core
    n_chips = n_cols // 2
    width = local_ref.shape[1] // n_cols

    def columns(c):
        return pl.ds(pl.multiple_of(c * width, width), width)

    def copy(src, dst, send, arrive, device):
        return pltpu.make_async_remote_copy(
            src_ref=src, dst_ref=dst, send_sem=send, recv_sem=arrive,
            device_id=device, device_id_type=pl.DeviceIdType.MESH,
        )

    def along(n, mine, step):
        def visit(i, carry):
            step(lax.rem(mine + 1 + i, n))
            return carry

        lax.fori_loop(0, n - 1, visit, 0)

    barrier = pltpu.get_barrier_semaphore()
    signal = functools.partial(pl.semaphore_signal, barrier, 1, device_id_type=pl.DeviceIdType.MESH)
    signal(device_id=(me_r, partner))
    along(n_chips, chip, lambda x: signal(device_id=(me_r, x * 2 + core)))
    along(n_rows, me_r, lambda r: signal(device_id=(r, me_c)))
    pl.semaphore_wait(barrier, n_chips + n_rows - 1)

    def swap(x):
        return copy(local_ref.at[:, columns(x * 2 + 1 - core)], from_core.at[x],
                    send_a.at[x], arrive_a.at[x], (me_r, partner))

    for x in range(n_chips):
        swap(x).start()
    for x in range(n_chips):
        swap(x).wait_recv()
    for x in range(n_chips):
        swap(x).wait_send()
    for x in range(n_chips):
        by_chip[x] = local_ref[:, columns(x * 2 + core)] + from_core[x]

    def share(x):
        return copy(by_chip.at[x], from_chip.at[chip], send_b.at[x], arrive_b.at[chip], (me_r, x * 2 + core))

    along(n_chips, chip, lambda x: share(x).start())
    from_chip[chip] = by_chip[chip]
    along(n_chips, chip, lambda x: copy(from_chip.at[x], from_chip.at[x], send_b.at[x], arrive_b.at[x],
                                        (me_r, x * 2 + core)).wait_recv())
    along(n_chips, chip, lambda x: share(x).wait_send())
    part[...] = jnp.sum(from_chip[...], axis=0).reshape(part.shape)

    def scatter(r):
        return copy(part.at[r], from_row.at[me_r], send_c.at[r], arrive_c.at[me_r], (r, me_c))

    along(n_rows, me_r, lambda r: scatter(r).start())
    from_row[me_r] = part[me_r]
    along(n_rows, me_r, lambda r: copy(from_row.at[r], from_row.at[r], send_c.at[r], arrive_c.at[r],
                                       (r, me_c)).wait_recv())
    along(n_rows, me_r, lambda r: scatter(r).wait_send())
    out_ref[...] = jnp.sum(from_row[...], axis=0)


def reduce_projection(partial):
    n_rows = lax.axis_size("rows")
    n_cols = lax.axis_size("cols")
    rank, grid = partial.shape
    width = grid // n_cols
    share = rank // n_rows
    n_chips = n_cols // 2
    return pl.pallas_call(
        functools.partial(projection_kernel, n_rows, n_cols),
        out_shape=jax.ShapeDtypeStruct((share, width), partial.dtype),
        in_specs=[pl.BlockSpec(memory_space=pltpu.VMEM)],
        out_specs=pl.BlockSpec(memory_space=pltpu.VMEM),
        scratch_shapes=[
            pltpu.VMEM((n_chips, rank, width), partial.dtype),
            pltpu.VMEM((n_chips, rank, width), partial.dtype),
            pltpu.VMEM((n_chips, rank, width), partial.dtype),
            pltpu.VMEM((n_rows, share, width), partial.dtype),
            pltpu.VMEM((n_rows, share, width), partial.dtype),
            pltpu.SemaphoreType.DMA((n_chips,)),
            pltpu.SemaphoreType.DMA((n_chips,)),
            pltpu.SemaphoreType.DMA((n_chips,)),
            pltpu.SemaphoreType.DMA((n_chips,)),
            pltpu.SemaphoreType.DMA((n_rows,)),
            pltpu.SemaphoreType.DMA((n_rows,)),
        ],
        compiler_params=pltpu.CompilerParams(collective_id=1, has_side_effects=True),
    )(partial)


def factor_inverse_block(gram, inverse_ref, work_ref):
    size = gram.shape[0]
    sub = lax.broadcasted_iota(jnp.int32, (size, size), 0)
    lane = lax.broadcasted_iota(jnp.int32, (size, size), 1)
    lane_row = lax.broadcasted_iota(jnp.int32, (1, size), 1)
    sub_col = lax.broadcasted_iota(jnp.int32, (size, 1), 0)

    def step(k, carry):
        row = work_ref[pl.ds(k, 1), :]
        work = work_ref[...]
        column = jnp.sum(jnp.where(lane == k, work, 0.0), axis=1, keepdims=True)
        pivot = jnp.sum(jnp.where(lane_row == k, row, 0.0), axis=1, keepdims=True)
        scale = lax.rsqrt(pivot)
        low_row = jnp.where(lane_row >= k, row * scale, 0.0)
        low_column = jnp.where(sub_col >= k, column * scale, 0.0)
        work_ref[...] = work - low_column * low_row
        inverse_row = inverse_ref[pl.ds(k, 1), :] * scale
        below = jnp.where(sub_col > k, low_column, 0.0)
        inverse = inverse_ref[...]
        inverse_ref[...] = jnp.where(sub == k, inverse_row, inverse - below * inverse_row)
        return carry

    work_ref[...] = gram
    inverse_ref[...] = jnp.where(sub == lane, 1.0, 0.0).astype(jnp.float32)
    lax.fori_loop(0, size, step, 0)


def nt(left, right):
    return lax.dot_general(
        left, right, (((1,), (1,)), ((), ())),
        precision=lax.Precision.HIGHEST, preferred_element_type=jnp.float32,
    )


def lower_inverse_kernel(gram_ref, out_ref, first, second, work_ref):
    half = gram_ref.shape[0] // 2
    factor_inverse_block(gram_ref[:half, :half], first, work_ref)
    inv11 = first[...]
    low21 = nt(gram_ref[half:, :half], inv11)
    factor_inverse_block(gram_ref[half:, half:] - nt(low21, low21), second, work_ref)
    inv22 = second[...]
    out_ref[:half, :half] = inv11
    out_ref[:half, half:] = jnp.zeros_like(inv11)
    out_ref[half:, :half] = -matmul(inv22, matmul(low21, inv11))
    out_ref[half:, half:] = inv22


def lower_inverse(gram):
    half = gram.shape[0] // 2
    block = pltpu.VMEM((half, half), gram.dtype)
    return pl.pallas_call(
        lower_inverse_kernel,
        out_shape=jax.ShapeDtypeStruct(gram.shape, gram.dtype),
        in_specs=[pl.BlockSpec(memory_space=pltpu.VMEM)],
        out_specs=pl.BlockSpec(memory_space=pltpu.VMEM),
        scratch_shapes=[block, block, block],
    )(gram)


def body(snapshots, test_matrix):
    n_rows = lax.axis_size("rows")
    n_cols = lax.axis_size("cols")
    rows_here = snapshots.shape[0]
    total_rows = rows_here * n_rows * n_cols
    sketch = jnp.dot(snapshots, test_matrix, preferred_element_type=jnp.float32)
    gram_local = cross_product(sketch, sketch)
    summed = all_reduce(gram_local)
    inverse_low = lower_inverse(summed)
    basis_full = lax.dot_general(
        sketch,
        inverse_low,
        (((1,), (1,)), ((), ())),
        precision=lax.Precision.HIGHEST,
        preferred_element_type=jnp.float32,
    ) * math.sqrt(total_rows)
    basis_half = basis_full.astype(jnp.bfloat16)
    partial = lax.dot_general(
        basis_half, snapshots, (((0,), (0,)), ((), ())), preferred_element_type=jnp.float32
    )
    projected = reduce_projection(partial)
    coeffs = projected * (1.0 / math.sqrt(total_rows))
    return (basis_full, coeffs)


def solution(mesh):
    placed = (P(("rows", "cols"), None), P())
    return jax.shard_map(
        body,
        mesh=mesh,
        in_specs=placed,
        out_specs=(P(("rows", "cols"), None), P("rows", "cols")),
        check_vma=False,
    )
```

```python
import functools
import math

import jax
import jax.numpy as jnp
from jax import lax
from jax.experimental import pallas as pl
from jax.experimental.pallas import tpu as pltpu
from jax.sharding import PartitionSpec as P


def cross_product(left, right):
    return lax.dot_general(
        left,
        right,
        (((0,), (0,)), ((), ())),
        precision=lax.Precision.HIGHEST,
        preferred_element_type=jnp.float32,
    )


def matmul(left, right):
    return jnp.dot(left, right, precision=lax.Precision.HIGHEST, preferred_element_type=jnp.float32)


def reduce_scatter(x, axis, n):
    chunks = x.reshape(n, x.shape[0] // n, *x.shape[1:])
    return lax.all_to_all(chunks, axis, 0, 0, tiled=True).sum(0)


def all_reduce_kernel(n_rows, n_cols, local_ref, out_ref, recv1, part, recv2, total, rows_in,
                      send1, arrive1, send2, arrive2, send3, arrive3, send4, arrive4):
    me_r = lax.axis_index("rows")
    me_c = lax.axis_index("cols")

    def along(n, mine, step):
        def visit(i, carry):
            step(lax.rem(mine + 1 + i, n))
            return carry

        lax.fori_loop(0, n - 1, visit, 0)

    def copy(src, dst, send, arrive, device):
        return pltpu.make_async_remote_copy(
            src_ref=src, dst_ref=dst, send_sem=send, recv_sem=arrive,
            device_id=device, device_id_type=pl.DeviceIdType.MESH,
        )

    barrier = pltpu.get_barrier_semaphore()
    along(n_cols, me_c, lambda c: pl.semaphore_signal(
        barrier, inc=1, device_id=(me_r, c), device_id_type=pl.DeviceIdType.MESH))
    along(n_rows, me_r, lambda r: pl.semaphore_signal(
        barrier, inc=1, device_id=(r, me_c), device_id_type=pl.DeviceIdType.MESH))
    pl.semaphore_wait(barrier, n_cols + n_rows - 2)

    def scatter1(c):
        return copy(local_ref.at[c], recv1.at[me_c], send1.at[c], arrive1.at[me_c], (me_r, c))

    along(n_cols, me_c, lambda c: scatter1(c).start())
    recv1[me_c] = local_ref[me_c]
    along(n_cols, me_c, lambda c: copy(recv1.at[c], recv1.at[c], send1.at[c], arrive1.at[c], (me_r, c)).wait_recv())
    along(n_cols, me_c, lambda c: scatter1(c).wait_send())
    summed = jnp.sum(recv1[...], axis=0)
    share = part.shape[1]
    for r in range(n_rows):
        part[r] = summed[r * share:(r + 1) * share]

    def scatter2(r):
        return copy(part.at[r], recv2.at[me_r], send2.at[r], arrive2.at[me_r], (r, me_c))

    along(n_rows, me_r, lambda r: scatter2(r).start())
    recv2[me_r] = part[me_r]
    along(n_rows, me_r, lambda r: copy(recv2.at[r], recv2.at[r], send2.at[r], arrive2.at[r], (r, me_c)).wait_recv())
    along(n_rows, me_r, lambda r: scatter2(r).wait_send())
    total[...] = jnp.sum(recv2[...], axis=0)

    def gather3(r):
        return copy(total, rows_in.at[me_r], send3.at[r], arrive3.at[me_r], (r, me_c))

    along(n_rows, me_r, lambda r: gather3(r).start())
    rows_in[me_r] = total[...]
    along(n_rows, me_r, lambda r: copy(rows_in.at[r], rows_in.at[r], send3.at[r], arrive3.at[r], (r, me_c)).wait_recv())
    along(n_rows, me_r, lambda r: gather3(r).wait_send())
    block = n_rows * share

    def rows_of(c):
        return pl.ds(pl.multiple_of(c * block, block), block)

    out_ref[rows_of(me_c), :] = jnp.concatenate([rows_in[r] for r in range(n_rows)], axis=0)

    def gather4(c):
        return copy(out_ref.at[rows_of(me_c)], out_ref.at[rows_of(me_c)], send4.at[c], arrive4.at[me_c], (me_r, c))

    along(n_cols, me_c, lambda c: gather4(c).start())
    along(n_cols, me_c, lambda c: copy(out_ref.at[rows_of(c)], out_ref.at[rows_of(c)], send4.at[c], arrive4.at[c], (me_r, c)).wait_recv())
    along(n_cols, me_c, lambda c: gather4(c).wait_send())


def all_reduce(x):
    n_rows = lax.axis_size("rows")
    n_cols = lax.axis_size("cols")
    rows, width = x.shape
    block = rows // n_cols
    out = pl.pallas_call(
        functools.partial(all_reduce_kernel, n_rows, n_cols),
        out_shape=jax.ShapeDtypeStruct((rows, width), x.dtype),
        in_specs=[pl.BlockSpec(memory_space=pltpu.VMEM)],
        out_specs=pl.BlockSpec(memory_space=pltpu.VMEM),
        scratch_shapes=[
            pltpu.VMEM((n_cols, block, width), x.dtype),
            pltpu.VMEM((n_rows, block // n_rows, width), x.dtype),
            pltpu.VMEM((n_rows, block // n_rows, width), x.dtype),
            pltpu.VMEM((block // n_rows, width), x.dtype),
            pltpu.VMEM((n_rows, block // n_rows, width), x.dtype),
            pltpu.SemaphoreType.DMA((n_cols,)),
            pltpu.SemaphoreType.DMA((n_cols,)),
            pltpu.SemaphoreType.DMA((n_rows,)),
            pltpu.SemaphoreType.DMA((n_rows,)),
            pltpu.SemaphoreType.DMA((n_rows,)),
            pltpu.SemaphoreType.DMA((n_rows,)),
            pltpu.SemaphoreType.DMA((n_cols,)),
            pltpu.SemaphoreType.DMA((n_cols,)),
        ],
        compiler_params=pltpu.CompilerParams(collective_id=0, has_side_effects=True),
    )(x.reshape(n_cols, block, width))
    return out


def projection_kernel(n_rows, n_cols, local_ref, out_ref, from_core, by_chip, from_chip, part, from_row,
                      send_a, arrive_a, send_b, arrive_b, send_c, arrive_c):
    me_r = lax.axis_index("rows")
    me_c = lax.axis_index("cols")
    core = lax.rem(me_c, 2)
    chip = me_c // 2
    partner = me_c + 1 - 2 * core
    n_chips = n_cols // 2
    width = local_ref.shape[1] // n_cols

    def columns(c):
        return pl.ds(pl.multiple_of(c * width, width), width)

    def copy(src, dst, send, arrive, device):
        return pltpu.make_async_remote_copy(
            src_ref=src, dst_ref=dst, send_sem=send, recv_sem=arrive,
            device_id=device, device_id_type=pl.DeviceIdType.MESH,
        )

    def along(n, mine, step):
        def visit(i, carry):
            step(lax.rem(mine + 1 + i, n))
            return carry

        lax.fori_loop(0, n - 1, visit, 0)

    barrier = pltpu.get_barrier_semaphore()
    signal = functools.partial(pl.semaphore_signal, barrier, 1, device_id_type=pl.DeviceIdType.MESH)
    signal(device_id=(me_r, partner))
    along(n_chips, chip, lambda x: signal(device_id=(me_r, x * 2 + core)))
    along(n_rows, me_r, lambda r: signal(device_id=(r, me_c)))
    pl.semaphore_wait(barrier, n_chips + n_rows - 1)

    def swap(x):
        return copy(local_ref.at[:, columns(x * 2 + 1 - core)], from_core.at[x],
                    send_a.at[x], arrive_a.at[x], (me_r, partner))

    def share(x):
        return copy(by_chip.at[x], from_chip.at[chip], send_b.at[x], arrive_b.at[chip], (me_r, x * 2 + core))

    order = [lax.rem(chip + 1 + i, n_chips) for i in range(n_chips)]
    for x in order:
        swap(x).start()
    for i, x in enumerate(order):
        swap(x).wait_recv()
        by_chip[x] = local_ref[:, columns(x * 2 + core)] + from_core[x]
        if i < n_chips - 1:
            share(x).start()
    for x in order:
        swap(x).wait_send()
    from_chip[chip] = by_chip[chip]
    along(n_chips, chip, lambda x: copy(from_chip.at[x], from_chip.at[x], send_b.at[x], arrive_b.at[x],
                                        (me_r, x * 2 + core)).wait_recv())
    along(n_chips, chip, lambda x: share(x).wait_send())
    part[...] = jnp.sum(from_chip[...], axis=0).reshape(part.shape)

    def scatter(r):
        return copy(part.at[r], from_row.at[me_r], send_c.at[r], arrive_c.at[me_r], (r, me_c))

    along(n_rows, me_r, lambda r: scatter(r).start())
    from_row[me_r] = part[me_r]
    along(n_rows, me_r, lambda r: copy(from_row.at[r], from_row.at[r], send_c.at[r], arrive_c.at[r],
                                       (r, me_c)).wait_recv())
    along(n_rows, me_r, lambda r: scatter(r).wait_send())
    out_ref[...] = jnp.sum(from_row[...], axis=0)


def reduce_projection(partial):
    n_rows = lax.axis_size("rows")
    n_cols = lax.axis_size("cols")
    rank, grid = partial.shape
    width = grid // n_cols
    share = rank // n_rows
    n_chips = n_cols // 2
    return pl.pallas_call(
        functools.partial(projection_kernel, n_rows, n_cols),
        out_shape=jax.ShapeDtypeStruct((share, width), partial.dtype),
        in_specs=[pl.BlockSpec(memory_space=pltpu.VMEM)],
        out_specs=pl.BlockSpec(memory_space=pltpu.VMEM),
        scratch_shapes=[
            pltpu.VMEM((n_chips, rank, width), partial.dtype),
            pltpu.VMEM((n_chips, rank, width), partial.dtype),
            pltpu.VMEM((n_chips, rank, width), partial.dtype),
            pltpu.VMEM((n_rows, share, width), partial.dtype),
            pltpu.VMEM((n_rows, share, width), partial.dtype),
            pltpu.SemaphoreType.DMA((n_chips,)),
            pltpu.SemaphoreType.DMA((n_chips,)),
            pltpu.SemaphoreType.DMA((n_chips,)),
            pltpu.SemaphoreType.DMA((n_chips,)),
            pltpu.SemaphoreType.DMA((n_rows,)),
            pltpu.SemaphoreType.DMA((n_rows,)),
        ],
        compiler_params=pltpu.CompilerParams(collective_id=1, has_side_effects=True),
    )(partial)


def factor_inverse_block(gram, inverse_ref, work_ref):
    size = gram.shape[0]
    sub = lax.broadcasted_iota(jnp.int32, (size, size), 0)
    lane = lax.broadcasted_iota(jnp.int32, (size, size), 1)
    lane_row = lax.broadcasted_iota(jnp.int32, (1, size), 1)
    sub_col = lax.broadcasted_iota(jnp.int32, (size, 1), 0)

    def step(k, carry):
        row = work_ref[pl.ds(k, 1), :]
        work = work_ref[...]
        column = jnp.sum(jnp.where(lane == k, work, 0.0), axis=1, keepdims=True)
        pivot = jnp.sum(jnp.where(lane_row == k, row, 0.0), axis=1, keepdims=True)
        scale = lax.rsqrt(pivot)
        low_row = jnp.where(lane_row >= k, row * scale, 0.0)
        low_column = jnp.where(sub_col >= k, column * scale, 0.0)
        work_ref[...] = work - low_column * low_row
        inverse_row = inverse_ref[pl.ds(k, 1), :] * scale
        below = jnp.where(sub_col > k, low_column, 0.0)
        inverse = inverse_ref[...]
        inverse_ref[...] = jnp.where(sub == k, inverse_row, inverse - below * inverse_row)
        return carry

    work_ref[...] = gram
    inverse_ref[...] = jnp.where(sub == lane, 1.0, 0.0).astype(jnp.float32)
    lax.fori_loop(0, size, step, 0)


def nt(left, right):
    return lax.dot_general(
        left, right, (((1,), (1,)), ((), ())),
        precision=lax.Precision.HIGHEST, preferred_element_type=jnp.float32,
    )


def lower_inverse_kernel(gram_ref, out_ref, first, second, work_ref):
    half = gram_ref.shape[0] // 2
    factor_inverse_block(gram_ref[:half, :half], first, work_ref)
    inv11 = first[...]
    low21 = nt(gram_ref[half:, :half], inv11)
    factor_inverse_block(gram_ref[half:, half:] - nt(low21, low21), second, work_ref)
    inv22 = second[...]
    out_ref[:half, :half] = inv11
    out_ref[:half, half:] = jnp.zeros_like(inv11)
    out_ref[half:, :half] = -matmul(inv22, matmul(low21, inv11))
    out_ref[half:, half:] = inv22


def lower_inverse(gram):
    half = gram.shape[0] // 2
    block = pltpu.VMEM((half, half), gram.dtype)
    return pl.pallas_call(
        lower_inverse_kernel,
        out_shape=jax.ShapeDtypeStruct(gram.shape, gram.dtype),
        in_specs=[pl.BlockSpec(memory_space=pltpu.VMEM)],
        out_specs=pl.BlockSpec(memory_space=pltpu.VMEM),
        scratch_shapes=[block, block, block],
    )(gram)


def body(snapshots, test_matrix):
    n_rows = lax.axis_size("rows")
    n_cols = lax.axis_size("cols")
    rows_here = snapshots.shape[0]
    total_rows = rows_here * n_rows * n_cols
    sketch = jnp.dot(snapshots, test_matrix, preferred_element_type=jnp.float32)
    gram_local = cross_product(sketch, sketch)
    summed = all_reduce(gram_local)
    inverse_low = lower_inverse(summed)
    basis_full = lax.dot_general(
        sketch,
        inverse_low,
        (((1,), (1,)), ((), ())),
        precision=lax.Precision.HIGHEST,
        preferred_element_type=jnp.float32,
    ) * math.sqrt(total_rows)
    basis_half = basis_full.astype(jnp.bfloat16)
    partial = lax.dot_general(
        basis_half, snapshots, (((0,), (0,)), ((), ())), preferred_element_type=jnp.float32
    )
    projected = reduce_projection(partial)
    coeffs = projected * (1.0 / math.sqrt(total_rows))
    return (basis_full, coeffs)


def solution(mesh):
    placed = (P(("rows", "cols"), None), P())
    return jax.shard_map(
        body,
        mesh=mesh,
        in_specs=placed,
        out_specs=(P(("rows", "cols"), None), P("rows", "cols")),
        check_vma=False,
    )
```

```python
import functools
import math

import jax
import jax.numpy as jnp
from jax import lax
from jax.experimental import pallas as pl
from jax.experimental.pallas import tpu as pltpu
from jax.sharding import PartitionSpec as P


def cross_product(left, right):
    return lax.dot_general(
        left,
        right,
        (((0,), (0,)), ((), ())),
        precision=lax.Precision.HIGHEST,
        preferred_element_type=jnp.float32,
    )


def matmul(left, right):
    return jnp.dot(left, right, precision=lax.Precision.HIGHEST, preferred_element_type=jnp.float32)


def reduce_scatter(x, axis, n):
    chunks = x.reshape(n, x.shape[0] // n, *x.shape[1:])
    return lax.all_to_all(chunks, axis, 0, 0, tiled=True).sum(0)


def all_reduce_kernel(n_rows, n_cols, local_ref, out_ref, recv1, part, recv2, total, rows_in,
                      send1, arrive1, send2, arrive2, send3, arrive3, send4, arrive4):
    me_r = lax.axis_index("rows")
    me_c = lax.axis_index("cols")

    def along(n, mine, step):
        def visit(i, carry):
            step(lax.rem(mine + 1 + i, n))
            return carry

        lax.fori_loop(0, n - 1, visit, 0)

    def copy(src, dst, send, arrive, device):
        return pltpu.make_async_remote_copy(
            src_ref=src, dst_ref=dst, send_sem=send, recv_sem=arrive,
            device_id=device, device_id_type=pl.DeviceIdType.MESH,
        )

    barrier = pltpu.get_barrier_semaphore()
    along(n_cols, me_c, lambda c: pl.semaphore_signal(
        barrier, inc=1, device_id=(me_r, c), device_id_type=pl.DeviceIdType.MESH))
    along(n_rows, me_r, lambda r: pl.semaphore_signal(
        barrier, inc=1, device_id=(r, me_c), device_id_type=pl.DeviceIdType.MESH))
    pl.semaphore_wait(barrier, n_cols + n_rows - 2)

    def scatter1(c):
        return copy(local_ref.at[c], recv1.at[me_c], send1.at[c], arrive1.at[me_c], (me_r, c))

    along(n_cols, me_c, lambda c: scatter1(c).start())
    recv1[me_c] = local_ref[me_c]
    along(n_cols, me_c, lambda c: copy(recv1.at[c], recv1.at[c], send1.at[c], arrive1.at[c], (me_r, c)).wait_recv())
    along(n_cols, me_c, lambda c: scatter1(c).wait_send())
    summed = jnp.sum(recv1[...], axis=0)
    share = part.shape[1]
    for r in range(n_rows):
        part[r] = summed[r * share:(r + 1) * share]

    def scatter2(r):
        return copy(part.at[r], recv2.at[me_r], send2.at[r], arrive2.at[me_r], (r, me_c))

    along(n_rows, me_r, lambda r: scatter2(r).start())
    recv2[me_r] = part[me_r]
    along(n_rows, me_r, lambda r: copy(recv2.at[r], recv2.at[r], send2.at[r], arrive2.at[r], (r, me_c)).wait_recv())
    along(n_rows, me_r, lambda r: scatter2(r).wait_send())
    total[...] = jnp.sum(recv2[...], axis=0)

    def gather3(r):
        return copy(total, rows_in.at[me_r], send3.at[r], arrive3.at[me_r], (r, me_c))

    along(n_rows, me_r, lambda r: gather3(r).start())
    rows_in[me_r] = total[...]
    along(n_rows, me_r, lambda r: copy(rows_in.at[r], rows_in.at[r], send3.at[r], arrive3.at[r], (r, me_c)).wait_recv())
    along(n_rows, me_r, lambda r: gather3(r).wait_send())
    block = n_rows * share

    def rows_of(c):
        return pl.ds(pl.multiple_of(c * block, block), block)

    out_ref[rows_of(me_c), :] = jnp.concatenate([rows_in[r] for r in range(n_rows)], axis=0)

    def gather4(c):
        return copy(out_ref.at[rows_of(me_c)], out_ref.at[rows_of(me_c)], send4.at[c], arrive4.at[me_c], (me_r, c))

    along(n_cols, me_c, lambda c: gather4(c).start())
    along(n_cols, me_c, lambda c: copy(out_ref.at[rows_of(c)], out_ref.at[rows_of(c)], send4.at[c], arrive4.at[c], (me_r, c)).wait_recv())
    along(n_cols, me_c, lambda c: gather4(c).wait_send())


def all_reduce(x):
    n_rows = lax.axis_size("rows")
    n_cols = lax.axis_size("cols")
    rows, width = x.shape
    block = rows // n_cols
    out = pl.pallas_call(
        functools.partial(all_reduce_kernel, n_rows, n_cols),
        out_shape=jax.ShapeDtypeStruct((rows, width), x.dtype),
        in_specs=[pl.BlockSpec(memory_space=pltpu.VMEM)],
        out_specs=pl.BlockSpec(memory_space=pltpu.VMEM),
        scratch_shapes=[
            pltpu.VMEM((n_cols, block, width), x.dtype),
            pltpu.VMEM((n_rows, block // n_rows, width), x.dtype),
            pltpu.VMEM((n_rows, block // n_rows, width), x.dtype),
            pltpu.VMEM((block // n_rows, width), x.dtype),
            pltpu.VMEM((n_rows, block // n_rows, width), x.dtype),
            pltpu.SemaphoreType.DMA((n_cols,)),
            pltpu.SemaphoreType.DMA((n_cols,)),
            pltpu.SemaphoreType.DMA((n_rows,)),
            pltpu.SemaphoreType.DMA((n_rows,)),
            pltpu.SemaphoreType.DMA((n_rows,)),
            pltpu.SemaphoreType.DMA((n_rows,)),
            pltpu.SemaphoreType.DMA((n_cols,)),
            pltpu.SemaphoreType.DMA((n_cols,)),
        ],
        compiler_params=pltpu.CompilerParams(collective_id=0, has_side_effects=True),
    )(x.reshape(n_cols, block, width))
    return out


def projection_kernel(n_rows, n_cols, factor, local_ref, out_ref, from_core, by_chip, from_chip, part, from_row,
                      send_a, arrive_a, send_b, arrive_b, send_c, arrive_c):
    me_r = lax.axis_index("rows")
    me_c = lax.axis_index("cols")
    core = lax.rem(me_c, 2)
    chip = me_c // 2
    partner = me_c + 1 - 2 * core
    n_chips = n_cols // 2
    width = local_ref.shape[1] // n_cols

    def columns(c):
        return pl.ds(pl.multiple_of(c * width, width), width)

    def copy(src, dst, send, arrive, device):
        return pltpu.make_async_remote_copy(
            src_ref=src, dst_ref=dst, send_sem=send, recv_sem=arrive,
            device_id=device, device_id_type=pl.DeviceIdType.MESH,
        )

    def along(n, mine, step):
        def visit(i, carry):
            step(lax.rem(mine + 1 + i, n))
            return carry

        lax.fori_loop(0, n - 1, visit, 0)

    barrier = pltpu.get_barrier_semaphore()
    signal = functools.partial(pl.semaphore_signal, barrier, 1, device_id_type=pl.DeviceIdType.MESH)
    signal(device_id=(me_r, partner))
    along(n_chips, chip, lambda x: signal(device_id=(me_r, x * 2 + core)))
    along(n_rows, me_r, lambda r: signal(device_id=(r, me_c)))
    pl.semaphore_wait(barrier, n_chips + n_rows - 1)

    def swap(x):
        return copy(local_ref.at[:, columns(x * 2 + 1 - core)], from_core.at[x],
                    send_a.at[x], arrive_a.at[x], (me_r, partner))

    def share(x):
        return copy(by_chip.at[x], from_chip.at[chip], send_b.at[x], arrive_b.at[chip], (me_r, x * 2 + core))

    order = [lax.rem(chip + 1 + i, n_chips) for i in range(n_chips)]
    for x in order:
        swap(x).start()
    for i, x in enumerate(order):
        swap(x).wait_recv()
        by_chip[x] = local_ref[:, columns(x * 2 + core)] + from_core[x]
        if i < n_chips - 1:
            share(x).start()
    for x in order:
        swap(x).wait_send()
    from_chip[chip] = by_chip[chip]
    along(n_chips, chip, lambda x: copy(from_chip.at[x], from_chip.at[x], send_b.at[x], arrive_b.at[x],
                                        (me_r, x * 2 + core)).wait_recv())
    along(n_chips, chip, lambda x: share(x).wait_send())
    part[...] = jnp.sum(from_chip[...], axis=0).reshape(part.shape)

    def scatter(r):
        return copy(part.at[r], from_row.at[me_r], send_c.at[r], arrive_c.at[me_r], (r, me_c))

    along(n_rows, me_r, lambda r: scatter(r).start())
    from_row[me_r] = part[me_r]
    along(n_rows, me_r, lambda r: copy(from_row.at[r], from_row.at[r], send_c.at[r], arrive_c.at[r],
                                       (r, me_c)).wait_recv())
    along(n_rows, me_r, lambda r: scatter(r).wait_send())
    out_ref[...] = jnp.sum(from_row[...], axis=0) * factor


def reduce_projection(partial, factor):
    n_rows = lax.axis_size("rows")
    n_cols = lax.axis_size("cols")
    rank, grid = partial.shape
    width = grid // n_cols
    share = rank // n_rows
    n_chips = n_cols // 2
    return pl.pallas_call(
        functools.partial(projection_kernel, n_rows, n_cols, factor),
        out_shape=jax.ShapeDtypeStruct((share, width), partial.dtype),
        in_specs=[pl.BlockSpec(memory_space=pltpu.VMEM)],
        out_specs=pl.BlockSpec(memory_space=pltpu.VMEM),
        scratch_shapes=[
            pltpu.VMEM((n_chips, rank, width), partial.dtype),
            pltpu.VMEM((n_chips, rank, width), partial.dtype),
            pltpu.VMEM((n_chips, rank, width), partial.dtype),
            pltpu.VMEM((n_rows, share, width), partial.dtype),
            pltpu.VMEM((n_rows, share, width), partial.dtype),
            pltpu.SemaphoreType.DMA((n_chips,)),
            pltpu.SemaphoreType.DMA((n_chips,)),
            pltpu.SemaphoreType.DMA((n_chips,)),
            pltpu.SemaphoreType.DMA((n_chips,)),
            pltpu.SemaphoreType.DMA((n_rows,)),
            pltpu.SemaphoreType.DMA((n_rows,)),
        ],
        compiler_params=pltpu.CompilerParams(collective_id=1, has_side_effects=True),
    )(partial)


def factor_inverse_block(gram, inverse_ref, work_ref):
    size = gram.shape[0]
    sub = lax.broadcasted_iota(jnp.int32, (size, size), 0)
    lane = lax.broadcasted_iota(jnp.int32, (size, size), 1)
    lane_row = lax.broadcasted_iota(jnp.int32, (1, size), 1)
    sub_col = lax.broadcasted_iota(jnp.int32, (size, 1), 0)

    def step(k, carry):
        row = work_ref[pl.ds(k, 1), :]
        work = work_ref[...]
        column = jnp.sum(jnp.where(lane == k, work, 0.0), axis=1, keepdims=True)
        pivot = jnp.sum(jnp.where(lane_row == k, row, 0.0), axis=1, keepdims=True)
        scale = lax.rsqrt(pivot)
        low_row = jnp.where(lane_row >= k, row * scale, 0.0)
        low_column = jnp.where(sub_col >= k, column * scale, 0.0)
        work_ref[...] = work - low_column * low_row
        inverse_row = inverse_ref[pl.ds(k, 1), :] * scale
        below = jnp.where(sub_col > k, low_column, 0.0)
        inverse = inverse_ref[...]
        inverse_ref[...] = jnp.where(sub == k, inverse_row, inverse - below * inverse_row)
        return carry

    work_ref[...] = gram
    inverse_ref[...] = jnp.where(sub == lane, 1.0, 0.0).astype(jnp.float32)
    lax.fori_loop(0, size, step, 0)


def nt(left, right):
    return lax.dot_general(
        left, right, (((1,), (1,)), ((), ())),
        precision=lax.Precision.HIGHEST, preferred_element_type=jnp.float32,
    )


def lower_inverse_kernel(gram_ref, out_ref, first, second, work_ref):
    half = gram_ref.shape[0] // 2
    factor_inverse_block(gram_ref[:half, :half], first, work_ref)
    inv11 = first[...]
    low21 = nt(gram_ref[half:, :half], inv11)
    factor_inverse_block(gram_ref[half:, half:] - nt(low21, low21), second, work_ref)
    inv22 = second[...]
    out_ref[:half, :half] = inv11
    out_ref[:half, half:] = jnp.zeros_like(inv11)
    out_ref[half:, :half] = -matmul(inv22, matmul(low21, inv11))
    out_ref[half:, half:] = inv22


def lower_inverse(gram):
    half = gram.shape[0] // 2
    block = pltpu.VMEM((half, half), gram.dtype)
    return pl.pallas_call(
        lower_inverse_kernel,
        out_shape=jax.ShapeDtypeStruct(gram.shape, gram.dtype),
        in_specs=[pl.BlockSpec(memory_space=pltpu.VMEM)],
        out_specs=pl.BlockSpec(memory_space=pltpu.VMEM),
        scratch_shapes=[block, block, block],
    )(gram)


def body(snapshots, test_matrix):
    n_rows = lax.axis_size("rows")
    n_cols = lax.axis_size("cols")
    rows_here = snapshots.shape[0]
    total_rows = rows_here * n_rows * n_cols
    sketch = jnp.dot(snapshots, test_matrix, preferred_element_type=jnp.float32)
    gram_local = cross_product(sketch, sketch)
    summed = all_reduce(gram_local)
    inverse_low = lower_inverse(summed)
    basis_full = lax.dot_general(
        sketch,
        inverse_low,
        (((1,), (1,)), ((), ())),
        precision=lax.Precision.HIGHEST,
        preferred_element_type=jnp.float32,
    ) * math.sqrt(total_rows)
    basis_half = basis_full.astype(jnp.bfloat16)
    partial = lax.dot_general(
        basis_half, snapshots, (((0,), (0,)), ((), ())), preferred_element_type=jnp.float32
    )
    coeffs = reduce_projection(partial, 1.0 / math.sqrt(total_rows))
    return (basis_full, coeffs)


def solution(mesh):
    placed = (P(("rows", "cols"), None), P())
    return jax.shard_map(
        body,
        mesh=mesh,
        in_specs=placed,
        out_specs=(P(("rows", "cols"), None), P("rows", "cols")),
        check_vma=False,
    )
```

```python
import functools
import math

import jax
import jax.numpy as jnp
from jax import lax
from jax.experimental import pallas as pl
from jax.experimental.pallas import tpu as pltpu
from jax.sharding import PartitionSpec as P


def cross_product(left, right):
    return lax.dot_general(
        left,
        right,
        (((0,), (0,)), ((), ())),
        precision=lax.Precision.HIGHEST,
        preferred_element_type=jnp.float32,
    )


def matmul(left, right):
    return jnp.dot(left, right, precision=lax.Precision.HIGHEST, preferred_element_type=jnp.float32)


def reduce_scatter(x, axis, n):
    chunks = x.reshape(n, x.shape[0] // n, *x.shape[1:])
    return lax.all_to_all(chunks, axis, 0, 0, tiled=True).sum(0)


def all_reduce_kernel(n_rows, n_cols, sketch_ref, out_ref, local_ref, recv1, part, recv2, total, rows_in,
                      send1, arrive1, send2, arrive2, send3, arrive3, send4, arrive4):
    me_r = lax.axis_index("rows")
    me_c = lax.axis_index("cols")

    def along(n, mine, step):
        def visit(i, carry):
            step(lax.rem(mine + 1 + i, n))
            return carry

        lax.fori_loop(0, n - 1, visit, 0)

    def copy(src, dst, send, arrive, device):
        return pltpu.make_async_remote_copy(
            src_ref=src, dst_ref=dst, send_sem=send, recv_sem=arrive,
            device_id=device, device_id_type=pl.DeviceIdType.MESH,
        )

    barrier = pltpu.get_barrier_semaphore()
    along(n_cols, me_c, lambda c: pl.semaphore_signal(
        barrier, inc=1, device_id=(me_r, c), device_id_type=pl.DeviceIdType.MESH))
    along(n_rows, me_r, lambda r: pl.semaphore_signal(
        barrier, inc=1, device_id=(r, me_c), device_id_type=pl.DeviceIdType.MESH))
    gram = cross_product(sketch_ref[...], sketch_ref[...])
    block = local_ref.shape[1]
    for c in range(n_cols):
        local_ref[c] = gram[c * block:(c + 1) * block]
    pl.semaphore_wait(barrier, n_cols + n_rows - 2)

    def scatter1(c):
        return copy(local_ref.at[c], recv1.at[me_c], send1.at[c], arrive1.at[me_c], (me_r, c))

    along(n_cols, me_c, lambda c: scatter1(c).start())
    recv1[me_c] = local_ref[me_c]
    along(n_cols, me_c, lambda c: copy(recv1.at[c], recv1.at[c], send1.at[c], arrive1.at[c], (me_r, c)).wait_recv())
    along(n_cols, me_c, lambda c: scatter1(c).wait_send())
    summed = jnp.sum(recv1[...], axis=0)
    share = part.shape[1]
    for r in range(n_rows):
        part[r] = summed[r * share:(r + 1) * share]

    def scatter2(r):
        return copy(part.at[r], recv2.at[me_r], send2.at[r], arrive2.at[me_r], (r, me_c))

    along(n_rows, me_r, lambda r: scatter2(r).start())
    recv2[me_r] = part[me_r]
    along(n_rows, me_r, lambda r: copy(recv2.at[r], recv2.at[r], send2.at[r], arrive2.at[r], (r, me_c)).wait_recv())
    along(n_rows, me_r, lambda r: scatter2(r).wait_send())
    total[...] = jnp.sum(recv2[...], axis=0)

    def gather3(r):
        return copy(total, rows_in.at[me_r], send3.at[r], arrive3.at[me_r], (r, me_c))

    along(n_rows, me_r, lambda r: gather3(r).start())
    rows_in[me_r] = total[...]
    along(n_rows, me_r, lambda r: copy(rows_in.at[r], rows_in.at[r], send3.at[r], arrive3.at[r], (r, me_c)).wait_recv())
    along(n_rows, me_r, lambda r: gather3(r).wait_send())
    block = n_rows * share

    def rows_of(c):
        return pl.ds(pl.multiple_of(c * block, block), block)

    out_ref[rows_of(me_c), :] = jnp.concatenate([rows_in[r] for r in range(n_rows)], axis=0)

    def gather4(c):
        return copy(out_ref.at[rows_of(me_c)], out_ref.at[rows_of(me_c)], send4.at[c], arrive4.at[me_c], (me_r, c))

    along(n_cols, me_c, lambda c: gather4(c).start())
    along(n_cols, me_c, lambda c: copy(out_ref.at[rows_of(c)], out_ref.at[rows_of(c)], send4.at[c], arrive4.at[c], (me_r, c)).wait_recv())
    along(n_cols, me_c, lambda c: gather4(c).wait_send())


def all_reduce(sketch):
    n_rows = lax.axis_size("rows")
    n_cols = lax.axis_size("cols")
    x = jax.ShapeDtypeStruct((sketch.shape[1], sketch.shape[1]), sketch.dtype)
    rows, width = x.shape
    block = rows // n_cols
    out = pl.pallas_call(
        functools.partial(all_reduce_kernel, n_rows, n_cols),
        out_shape=jax.ShapeDtypeStruct((rows, width), x.dtype),
        in_specs=[pl.BlockSpec(memory_space=pltpu.VMEM)],
        out_specs=pl.BlockSpec(memory_space=pltpu.VMEM),
        scratch_shapes=[
            pltpu.VMEM((n_cols, block, width), x.dtype),
            pltpu.VMEM((n_cols, block, width), x.dtype),
            pltpu.VMEM((n_rows, block // n_rows, width), x.dtype),
            pltpu.VMEM((n_rows, block // n_rows, width), x.dtype),
            pltpu.VMEM((block // n_rows, width), x.dtype),
            pltpu.VMEM((n_rows, block // n_rows, width), x.dtype),
            pltpu.SemaphoreType.DMA((n_cols,)),
            pltpu.SemaphoreType.DMA((n_cols,)),
            pltpu.SemaphoreType.DMA((n_rows,)),
            pltpu.SemaphoreType.DMA((n_rows,)),
            pltpu.SemaphoreType.DMA((n_rows,)),
            pltpu.SemaphoreType.DMA((n_rows,)),
            pltpu.SemaphoreType.DMA((n_cols,)),
            pltpu.SemaphoreType.DMA((n_cols,)),
        ],
        compiler_params=pltpu.CompilerParams(collective_id=0, has_side_effects=True),
    )(sketch)
    return out


def projection_kernel(n_rows, n_cols, local_ref, out_ref, from_core, by_chip, from_chip, part, from_row,
                      send_a, arrive_a, send_b, arrive_b, send_c, arrive_c):
    me_r = lax.axis_index("rows")
    me_c = lax.axis_index("cols")
    core = lax.rem(me_c, 2)
    chip = me_c // 2
    partner = me_c + 1 - 2 * core
    n_chips = n_cols // 2
    width = local_ref.shape[1] // n_cols

    def columns(c):
        return pl.ds(pl.multiple_of(c * width, width), width)

    def copy(src, dst, send, arrive, device):
        return pltpu.make_async_remote_copy(
            src_ref=src, dst_ref=dst, send_sem=send, recv_sem=arrive,
            device_id=device, device_id_type=pl.DeviceIdType.MESH,
        )

    def along(n, mine, step):
        def visit(i, carry):
            step(lax.rem(mine + 1 + i, n))
            return carry

        lax.fori_loop(0, n - 1, visit, 0)

    barrier = pltpu.get_barrier_semaphore()
    signal = functools.partial(pl.semaphore_signal, barrier, 1, device_id_type=pl.DeviceIdType.MESH)
    signal(device_id=(me_r, partner))
    along(n_chips, chip, lambda x: signal(device_id=(me_r, x * 2 + core)))
    along(n_rows, me_r, lambda r: signal(device_id=(r, me_c)))
    pl.semaphore_wait(barrier, n_chips + n_rows - 1)

    def swap(x):
        return copy(local_ref.at[:, columns(x * 2 + 1 - core)], from_core.at[x],
                    send_a.at[x], arrive_a.at[x], (me_r, partner))

    def share(x):
        return copy(by_chip.at[x], from_chip.at[chip], send_b.at[x], arrive_b.at[chip], (me_r, x * 2 + core))

    order = [lax.rem(chip + 1 + i, n_chips) for i in range(n_chips)]
    for x in order:
        swap(x).start()
    for i, x in enumerate(order):
        swap(x).wait_recv()
        by_chip[x] = local_ref[:, columns(x * 2 + core)] + from_core[x]
        if i < n_chips - 1:
            share(x).start()
    for x in order:
        swap(x).wait_send()
    from_chip[chip] = by_chip[chip]
    along(n_chips, chip, lambda x: copy(from_chip.at[x], from_chip.at[x], send_b.at[x], arrive_b.at[x],
                                        (me_r, x * 2 + core)).wait_recv())
    along(n_chips, chip, lambda x: share(x).wait_send())
    part[...] = jnp.sum(from_chip[...], axis=0).reshape(part.shape)

    def scatter(r):
        return copy(part.at[r], from_row.at[me_r], send_c.at[r], arrive_c.at[me_r], (r, me_c))

    along(n_rows, me_r, lambda r: scatter(r).start())
    from_row[me_r] = part[me_r]
    along(n_rows, me_r, lambda r: copy(from_row.at[r], from_row.at[r], send_c.at[r], arrive_c.at[r],
                                       (r, me_c)).wait_recv())
    along(n_rows, me_r, lambda r: scatter(r).wait_send())
    out_ref[...] = jnp.sum(from_row[...], axis=0)


def reduce_projection(partial):
    n_rows = lax.axis_size("rows")
    n_cols = lax.axis_size("cols")
    rank, grid = partial.shape
    width = grid // n_cols
    share = rank // n_rows
    n_chips = n_cols // 2
    return pl.pallas_call(
        functools.partial(projection_kernel, n_rows, n_cols),
        out_shape=jax.ShapeDtypeStruct((share, width), partial.dtype),
        in_specs=[pl.BlockSpec(memory_space=pltpu.VMEM)],
        out_specs=pl.BlockSpec(memory_space=pltpu.VMEM),
        scratch_shapes=[
            pltpu.VMEM((n_chips, rank, width), partial.dtype),
            pltpu.VMEM((n_chips, rank, width), partial.dtype),
            pltpu.VMEM((n_chips, rank, width), partial.dtype),
            pltpu.VMEM((n_rows, share, width), partial.dtype),
            pltpu.VMEM((n_rows, share, width), partial.dtype),
            pltpu.SemaphoreType.DMA((n_chips,)),
            pltpu.SemaphoreType.DMA((n_chips,)),
            pltpu.SemaphoreType.DMA((n_chips,)),
            pltpu.SemaphoreType.DMA((n_chips,)),
            pltpu.SemaphoreType.DMA((n_rows,)),
            pltpu.SemaphoreType.DMA((n_rows,)),
        ],
        compiler_params=pltpu.CompilerParams(collective_id=1, has_side_effects=True),
    )(partial)


def factor_inverse_block(gram, inverse_ref, work_ref):
    size = gram.shape[0]
    sub = lax.broadcasted_iota(jnp.int32, (size, size), 0)
    lane = lax.broadcasted_iota(jnp.int32, (size, size), 1)
    lane_row = lax.broadcasted_iota(jnp.int32, (1, size), 1)
    sub_col = lax.broadcasted_iota(jnp.int32, (size, 1), 0)

    def step(k, carry):
        row = work_ref[pl.ds(k, 1), :]
        work = work_ref[...]
        column = jnp.sum(jnp.where(lane == k, work, 0.0), axis=1, keepdims=True)
        pivot = jnp.sum(jnp.where(lane_row == k, row, 0.0), axis=1, keepdims=True)
        scale = lax.rsqrt(pivot)
        low_row = jnp.where(lane_row >= k, row * scale, 0.0)
        low_column = jnp.where(sub_col >= k, column * scale, 0.0)
        work_ref[...] = work - low_column * low_row
        inverse_row = inverse_ref[pl.ds(k, 1), :] * scale
        below = jnp.where(sub_col > k, low_column, 0.0)
        inverse = inverse_ref[...]
        inverse_ref[...] = jnp.where(sub == k, inverse_row, inverse - below * inverse_row)
        return carry

    work_ref[...] = gram
    inverse_ref[...] = jnp.where(sub == lane, 1.0, 0.0).astype(jnp.float32)
    lax.fori_loop(0, size, step, 0)


def nt(left, right):
    return lax.dot_general(
        left, right, (((1,), (1,)), ((), ())),
        precision=lax.Precision.HIGHEST, preferred_element_type=jnp.float32,
    )


def lower_inverse_kernel(gram_ref, out_ref, first, second, work_ref):
    half = gram_ref.shape[0] // 2
    factor_inverse_block(gram_ref[:half, :half], first, work_ref)
    inv11 = first[...]
    low21 = nt(gram_ref[half:, :half], inv11)
    factor_inverse_block(gram_ref[half:, half:] - nt(low21, low21), second, work_ref)
    inv22 = second[...]
    out_ref[:half, :half] = inv11
    out_ref[:half, half:] = jnp.zeros_like(inv11)
    out_ref[half:, :half] = -matmul(inv22, matmul(low21, inv11))
    out_ref[half:, half:] = inv22


def lower_inverse(gram):
    half = gram.shape[0] // 2
    block = pltpu.VMEM((half, half), gram.dtype)
    return pl.pallas_call(
        lower_inverse_kernel,
        out_shape=jax.ShapeDtypeStruct(gram.shape, gram.dtype),
        in_specs=[pl.BlockSpec(memory_space=pltpu.VMEM)],
        out_specs=pl.BlockSpec(memory_space=pltpu.VMEM),
        scratch_shapes=[block, block, block],
    )(gram)


def body(snapshots, test_matrix):
    n_rows = lax.axis_size("rows")
    n_cols = lax.axis_size("cols")
    rows_here = snapshots.shape[0]
    total_rows = rows_here * n_rows * n_cols
    sketch = jnp.dot(snapshots, test_matrix, preferred_element_type=jnp.float32)
    summed = all_reduce(sketch)
    inverse_low = lower_inverse(summed)
    basis_full = lax.dot_general(
        sketch,
        inverse_low,
        (((1,), (1,)), ((), ())),
        precision=lax.Precision.HIGHEST,
        preferred_element_type=jnp.float32,
    ) * math.sqrt(total_rows)
    basis_half = basis_full.astype(jnp.bfloat16)
    partial = lax.dot_general(
        basis_half, snapshots, (((0,), (0,)), ((), ())), preferred_element_type=jnp.float32
    )
    projected = reduce_projection(partial)
    coeffs = projected * (1.0 / math.sqrt(total_rows))
    return (basis_full, coeffs)


def solution(mesh):
    placed = (P(("rows", "cols"), None), P())
    return jax.shard_map(
        body,
        mesh=mesh,
        in_specs=placed,
        out_specs=(P(("rows", "cols"), None), P("rows", "cols")),
        check_vma=False,
    )
```
